32 devices in a mesh: sets: 16 (over z, x, core), tp: 2 (over y).
Axes of the slice: x: 2, y: 2, z: 4, core: 2. Of those that a mesh axis runs over, the one named last changes fastest.
Arguments:
- latents: bfloat16 [16384, 1024], P(('sets', 'tp')), may hold values from -6 to 6
- inputs: bfloat16 [16384, 1024], P(('sets', 'tp')), may hold values from -6 to 6
- neighbours: int32 [128, 512], P('sets'), may hold values from 0 to 1023
- key_counts: int32 [128], P('sets'), may hold values from 65 to 512, as said below
- filled: int32 [16], P('sets'), may hold values from 2 to 8, as said below
- cotangent: bfloat16 [16384, 1024], P(('sets', 'tp')), may hold values from -6 to 6
- cross_gain: float32 [1024], replicated, may hold values from 0.1 to 1.9
- cross_query: bfloat16 [1024, 1024], P(None, 'tp'), may hold values from -0.1875 to 0.1875
- cross_key: bfloat16 [1024, 1024], P(None, 'tp'), may hold values from -0.1875 to 0.1875
- cross_value: bfloat16 [1024, 1024], P(None, 'tp'), may hold values from -0.1875 to 0.1875
- cross_output: bfloat16 [1024, 1024], P('tp'), may hold values from -0.75 to 0.75
- self_gain: float32 [1024], replicated, may hold values from 0.1 to 1.9
- self_query: bfloat16 [1024, 1024], P(None, 'tp'), may hold values from -0.1875 to 0.1875
- self_key: bfloat16 [1024, 1024], P(None, 'tp'), may hold values from -0.1875 to 0.1875
- self_value: bfloat16 [1024, 1024], P(None, 'tp'), may hold values from -0.1875 to 0.1875
- self_output: bfloat16 [1024, 1024], P('tp'), may hold values from -0.5 to 0.5
- feed_gain: float32 [1024], replicated, may hold values from 0.1 to 1.9
- feed_up: bfloat16 [1024, 4096], P(None, 'tp'), may hold values from -0.1875 to 0.1875
- feed_down: bfloat16 [4096, 1024], P('tp'), may hold values from -0.09375 to 0.09375
Outputs:
- latents_out: bfloat16 [16384, 1024], P(('sets', 'tp'))
- latent_grad: float32 [16384, 1024], P(('sets', 'tp'))
- input_grad: float32 [16384, 1024], P(('sets', 'tp'))
- grad_cross_gain: float32 [1024], replicated
- grad_cross_query: float32 [1024, 1024], P(None, 'tp')
- grad_cross_key: float32 [1024, 1024], P(None, 'tp')
- grad_cross_value: float32 [1024, 1024], P(None, 'tp')
- grad_cross_output: float32 [1024, 1024], P('tp')
- grad_self_gain: float32 [1024], replicated
- grad_self_query: float32 [1024, 1024], P(None, 'tp')
- grad_self_key: float32 [1024, 1024], P(None, 'tp')
- grad_self_value: float32 [1024, 1024], P(None, 'tp')
- grad_self_output: float32 [1024, 1024], P('tp')
- grad_feed_gain: float32 [1024], replicated
- grad_feed_up: float32 [1024, 4096], P(None, 'tp')
- grad_feed_down: float32 [4096, 1024], P('tp')
- penalty: float32 [], replicated
The draws below stay inside these ranges and needn't reach their ends.
Inputs may be any that keep to these rules, and one draw needn't show every extreme that they name: `neighbours`: each entry is a row of the group's own point set, counted from that set's first input embedding. Only the first key_counts[g] entries of group g's neighbour list count; some group has all 512. Groups of point set s numbered filled[s] and above are padding; some point set is full.
All inputs are finite; a program needn't handle non-finite values.
Results may differ from the reference program's by a relative error of at most 0.035.
Values may be sent and summed in bfloat16 or wider, within the bound.
No kernel may reach another device: no remote copies, remote signals or barrier semaphores. Data moves between devices by JAX's collectives and lax.ppermute only.
A program may use at most 256 MiB of HBM per device.

```python
import math
import jax
import jax.numpy as jnp
from jax import lax

D = 1024
HEADS = 8
HEAD_DIM = 128
FF = 4096
GROUP = 128
KEYS = 512
SETS = 16
GROUPS_SET = 8
GROUPS = 128
LATENTS = 16384
IN_SET = 1024
INPUTS = 16384
N_SETS = 16


def draw_key_counts(key, part):
    first_key, second_key = jax.random.split(jax.random.fold_in(key, 11))
    divisor = jax.random.randint(first_key, (GROUPS,), 8, 64)
    drawn = KEYS * 8 // divisor
    chosen = jax.random.randint(second_key, (), 0, GROUPS)
    return drawn.at[chosen].set(KEYS).astype(jnp.int32)


def draw_filled(key, part):
    first_key, second_key = jax.random.split(jax.random.fold_in(key, 23))
    drawn = jax.random.randint(first_key, (SETS,), max(1, GROUPS_SET // 4), GROUPS_SET + 1)
    chosen = jax.random.randint(second_key, (), 0, SETS)
    return drawn.at[chosen].set(GROUPS_SET).astype(jnp.int32)


def touch_ends(entries, stream_key, smallest, largest):
    extent = entries.shape
    index_at = [jax.random.randint(jax.random.fold_in(stream_key, axis), (), 0, extent[axis]) for axis in range(len(extent))]
    entries = entries.at[tuple(index_at)].set(smallest)
    longest = extent.index(max(extent))
    index_at[longest] = (index_at[longest] + 1) % extent[longest]
    return entries.at[tuple(index_at)].set(largest)


def block_levels(key, extent, cuts, low, largest):
    level = 1.0
    for position, shards_of in cuts:
        heights = jax.random.uniform(jax.random.fold_in(jax.random.fold_in(key, 6), position), (shards_of,), jnp.float32, low / len(cuts), largest / len(cuts))
        level = level * jnp.repeat(jnp.exp(heights), extent[position] // shards_of).reshape((-1,) + (1,) * (len(extent) - 1 - position))
    return level


def gaussian(own_key, dims, spread, reach, cuts=(), kind=jnp.bfloat16):
    values = jax.random.normal(own_key, dims, jnp.float32) * spread
    if len(cuts) > 0:
        values = block_levels(own_key, dims, cuts, -0.22, 0.18) * values
    return jnp.clip(values, min=-reach, max=reach).astype(kind)


def setup_inputs(seed: int = 0) -> dict:
    seeds = jax.random.split(jax.random.key(seed), 20)
    return {
        "latents": gaussian(seeds[0], (LATENTS, D), 1.0, 6.0, ((0, 32),)),
        "inputs": gaussian(seeds[1], (INPUTS, D), 1.0, 6.0, ((0, 32),)),
        "neighbours": touch_ends(jax.random.randint(seeds[2], (GROUPS, KEYS), 0, IN_SET), jax.random.fold_in(seeds[2], 1), 0, IN_SET - 1).astype(jnp.int32),
        "key_counts": draw_key_counts(jax.random.fold_in(seeds[19], 71), 0),
        "filled": draw_filled(jax.random.fold_in(seeds[19], 71), 0),
        "cotangent": gaussian(seeds[5], (LATENTS, D), 1.0, 6.0, ((0, 32),)),
        "cross_gain": jnp.clip(1.0 + 0.18 * jax.random.normal(seeds[6], (D,), jnp.float32), 0.1, 1.9),
        "cross_query": gaussian(seeds[7], (D, D), D ** -0.5, 0.1875, ((1, 2),)),
        "cross_key": gaussian(seeds[8], (D, D), D ** -0.5, 0.1875, ((1, 2),)),
        "cross_value": gaussian(seeds[9], (D, D), D ** -0.5, 0.1875, ((1, 2),)),
        "cross_output": gaussian(seeds[10], (D, D), (D // 16) ** -0.5, 0.75, ((0, 2),)),
        "self_gain": jnp.clip(1.0 + 0.18 * jax.random.normal(seeds[11], (D,), jnp.float32), 0.1, 1.9),
        "self_query": gaussian(seeds[12], (D, D), D ** -0.5, 0.1875, ((1, 2),)),
        "self_key": gaussian(seeds[13], (D, D), D ** -0.5, 0.1875, ((1, 2),)),
        "self_value": gaussian(seeds[14], (D, D), D ** -0.5, 0.1875, ((1, 2),)),
        "self_output": gaussian(seeds[15], (D, D), (D // 8) ** -0.5, 0.5, ((0, 2),)),
        "feed_gain": jnp.clip(1.0 + 0.18 * jax.random.normal(seeds[16], (D,), jnp.float32), 0.1, 1.9),
        "feed_up": gaussian(seeds[17], (D, FF), D ** -0.5, 0.1875, ((1, 2),)),
        "feed_down": gaussian(seeds[18], (FF, D), FF ** -0.5, 0.09375, ((0, 2),)),
    }


@jax.custom_vjp
def low(v):
    return lax.optimization_barrier(v.astype(jnp.bfloat16)).astype(jnp.float32)

@jax.custom_vjp
def low_back(v):
    return v

def low_keep(v):
    return (low(v), None)

def low_pass(kept, grad):
    return (grad,)

def back_keep(v):
    return (v, None)

def back_low(kept, grad):
    return (low(grad),)
low.defvjp(low_keep, low_pass)
low_back.defvjp(back_keep, back_low)
epsilon = 1e-05
masked_score = -1e+30
gelu_factor = 0.7978845608028654
highest = lax.Precision.HIGHEST

def gelu_curve(values):
    return 0.5 * values * (1.0 + jnp.tanh(gelu_factor * (values + 0.044715 * values * values * values)))

def product(left_rows, right_rows):
    return jnp.dot(left_rows, right_rows, precision=highest)

def layer_norm(values, gain):
    average = lax.optimization_barrier(jnp.mean(values, axis=-1, keepdims=True))
    centred = values - average
    variance = lax.optimization_barrier(jnp.mean(centred * centred, axis=-1, keepdims=True))
    return centred * lax.rsqrt(variance + epsilon) * gain

def attend(queries, keys, values, valid):
    scores = jnp.einsum('gqhd,gkhd->ghqk', queries, keys, precision=highest) * (1.0 / math.sqrt(HEAD_DIM))
    scores = low_back(scores)
    if valid is not None:
        scores = jnp.where(valid[:, None, None, :], scores, masked_score)
    row_top = lax.optimization_barrier(jnp.max(scores, axis=-1, keepdims=True))
    raised = jnp.exp(scores - row_top)
    weights_soft = low(raised / lax.optimization_barrier(jnp.sum(raised, axis=-1, keepdims=True)))
    return jnp.einsum('ghqk,gkhd->gqhd', weights_soft, values, precision=highest)

def block_forward(state_rows, embedded, chosen, counts, filled_count, weights):
    cross_gain, cross_query, cross_key, cross_value, cross_output, self_gain, self_query, self_key, self_value, self_output, feed_gain, feed_up, feed_down = weights
    row_total = state_rows.shape[0]
    group_total = row_total // GROUP
    alive_groups = (jnp.arange(group_total, dtype=jnp.int32) < filled_count).astype(jnp.float32)
    alive_rows = jnp.repeat(alive_groups, GROUP)[:, None]
    normed = low(layer_norm(state_rows, cross_gain))
    queries = low(low_back(product(normed, cross_query)))
    key_table = low(low_back(product(embedded, cross_key)))
    value_table = low(low_back(product(embedded, cross_value)))
    picked_keys = key_table[chosen].reshape(group_total, KEYS, HEADS, HEAD_DIM)
    picked_values = value_table[chosen].reshape(group_total, KEYS, HEADS, HEAD_DIM)
    valid = jnp.arange(KEYS, dtype=jnp.int32)[None, :] < counts[:, None]
    attended = attend(queries.reshape(group_total, GROUP, HEADS, HEAD_DIM), picked_keys, picked_values, valid)
    attended = low(low_back(attended.reshape(row_total, D)))
    branch = low_back(product(attended, cross_output))
    after_cross = state_rows + alive_rows * branch
    normed = low(layer_norm(after_cross, self_gain))
    queries = low(low_back(product(normed, self_query))).reshape(group_total, GROUP, HEADS, HEAD_DIM)
    keys_self = low(low_back(product(normed, self_key))).reshape(group_total, GROUP, HEADS, HEAD_DIM)
    values_self = low(low_back(product(normed, self_value))).reshape(group_total, GROUP, HEADS, HEAD_DIM)
    attended = attend(queries, keys_self, values_self, None)
    attended = low(low_back(attended.reshape(row_total, D)))
    branch = low_back(product(attended, self_output))
    after_self = after_cross + alive_rows * branch
    normed = low(layer_norm(after_self, feed_gain))
    hidden = low_back(product(normed, feed_up))
    activated = low(gelu_curve(hidden))
    branch = low_back(product(activated, feed_down))
    return after_self + alive_rows * branch

def add_pair(first_value, second_value):
    return first_value + second_value

def reference(latents, inputs, neighbours, key_counts, filled, cotangent, cross_gain, cross_query, cross_key, cross_value, cross_output, self_gain, self_query, self_key, self_value, self_output, feed_gain, feed_up, feed_down):
    weights = tuple((matrix.astype(jnp.float32) for matrix in (cross_gain, cross_query, cross_key, cross_value, cross_output, self_gain, self_query, self_key, self_value, self_output, feed_gain, feed_up, feed_down)))
    per_set = (latents.astype(jnp.float32).reshape(N_SETS, -1, D), inputs.astype(jnp.float32).reshape(N_SETS, -1, D), neighbours.reshape(N_SETS, -1, KEYS), key_counts.reshape(N_SETS, -1), filled, cotangent.astype(jnp.float32).reshape(N_SETS, -1, D))
    zero_grads = tuple((jnp.zeros_like(matrix) for matrix in weights))

    def one_set(totals, pieces):
        state_rows, embedded, chosen, counts, filled_count, grad_out = pieces

        def forward(state_in, embedded_in, weights_in):
            return block_forward(state_in, embedded_in, chosen, counts, filled_count, weights_in)
        output, pull = jax.vjp(forward, state_rows, embedded, weights)
        grad_state, grad_embedded, grad_weights = pull(grad_out)
        totals = tuple((add_pair(total_grad, new_grad) for total_grad, new_grad in zip(totals, grad_weights)))
        group_total = output.shape[0] // GROUP
        group_rms = jnp.sqrt(lax.optimization_barrier(jnp.mean((output * output).reshape(group_total, -1), axis=1)))
        alive_groups = (jnp.arange(group_total, dtype=jnp.int32) < filled_count).astype(jnp.float32)
        return (totals, (output, grad_state, grad_embedded, jnp.sum(group_rms * alive_groups)))
    totals, (outputs, grad_states, grad_inputs, terms) = lax.scan(one_set, zero_grads, per_set)
    penalty = jnp.sum(terms) / GROUPS
    return (outputs.reshape(-1, D).astype(jnp.bfloat16), grad_states.reshape(-1, D), grad_inputs.reshape(-1, D), totals[0], totals[1], totals[2], totals[3], totals[4], totals[5], totals[6], totals[7], totals[8], totals[9], totals[10], totals[11], totals[12], penalty)
```

```python
import functools
import math

import jax
import jax.numpy as jnp
from jax import lax
from jax.experimental import pallas as pl
from jax.experimental.pallas import tpu as pltpu
from jax.sharding import PartitionSpec as P

HEAD_DIM = 128
GROUP = 128

epsilon = 1e-05
masked_score = -1e30
gelu_factor = 0.7978845608028654
gelu_cubic = 0.044715
log2_e = 1.4426950408889634
vmem_bytes = 60 * 1024 * 1024


def project(left_rows, right_rows):
    return jnp.dot(left_rows, right_rows, preferred_element_type=jnp.float32)


def times_transposed(left_rows, right_rows):
    return lax.dot_general(
        left_rows, right_rows, (((1,), (1,)), ((), ())), preferred_element_type=jnp.float32
    )


def transposed_times(left_rows, right_rows):
    return lax.dot_general(
        left_rows, right_rows, (((0,), (0,)), ((), ())), preferred_element_type=jnp.float32
    )


def norm_forward(values, gain):
    average = jnp.mean(values, axis=1, keepdims=True)
    centred = values - average
    variance = jnp.mean(centred * centred, axis=1, keepdims=True)
    inverse = lax.rsqrt(variance + epsilon)
    unit_rows = centred * inverse
    return (unit_rows, inverse, (unit_rows * gain).astype(jnp.bfloat16))


def norm_backward(grad_normed, unit_rows, inverse, gain):
    scaled = grad_normed * gain
    first_mean = jnp.mean(scaled, axis=1, keepdims=True)
    second_mean = jnp.mean(scaled * unit_rows, axis=1, keepdims=True)
    grad_rows = inverse * (scaled - first_mean - unit_rows * second_mean)
    return (grad_rows, jnp.sum(grad_normed * unit_rows, axis=0))


def from_peer(block, step):
    count = lax.axis_size("tp")
    return lax.ppermute(block, "tp", [(source, (source - step) % count) for source in range(count)])


def to_peer(block, step):
    count = lax.axis_size("tp")
    return lax.ppermute(block, "tp", [(source, (source + step) % count) for source in range(count)])


def gather_blocks(block):
    return [block] + [from_peer(block, step) for step in range(1, lax.axis_size("tp"))]


def sum_blocks(make_partial):
    received = [
        to_peer(make_partial(step).astype(jnp.bfloat16), step)
        for step in range(1, lax.axis_size("tp"))
    ]
    total = make_partial(0)
    for term in received:
        total = total + term.astype(jnp.float32)
    return total


def swap_sets(block, bit):
    count = lax.axis_size("sets")
    return lax.ppermute(block, "sets", [(source, source ^ (1 << bit)) for source in range(count)])


def set_bit(bit):
    return (lax.axis_index("sets") >> bit) & 1


def halves(block, bit):
    half = block.shape[0] // 2
    mine = set_bit(bit)
    kept = lax.dynamic_slice_in_dim(block, mine * half, half, 0)
    sent = lax.dynamic_slice_in_dim(block, (1 - mine) * half, half, 0)
    return (kept, sent)


def add_pair(kept, received):
    return (kept.astype(jnp.float32) + received.astype(jnp.float32)).astype(jnp.bfloat16)


def scatter_sets(block, bits):
    for bit in bits:
        kept, sent = halves(block, bit)
        block = add_pair(kept, swap_sets(sent, bit))
    return block


def spread_sets(block, bits):
    for bit in reversed(bits):
        received = swap_sets(block, bit)
        first = set_bit(bit) == 0
        block = jnp.concatenate(
            [jnp.where(first, block, received), jnp.where(first, received, block)], axis=0
        )
    return block


def all_bits():
    return list(range(int(math.log2(lax.axis_size("sets")))))


def sum_sets(block, bits):
    return spread_sets(scatter_sets(block.astype(jnp.bfloat16), bits), bits).astype(jnp.float32)


def sum_everywhere(block):
    for bit in all_bits():
        block = block + swap_sets(block, bit)
    count = lax.axis_size("tp")
    step = 1
    while step < count:
        block = block + lax.ppermute(
            block, "tp", [(source, source ^ step) for source in range(count)]
        )
        step *= 2
    return block


def multiplicity_kernel(chosen_ref, out_ref):
    row_count = out_ref.shape[0]
    group_count, key_count = chosen_ref.shape
    row_ids = lax.broadcasted_iota(jnp.int32, (row_count, key_count), 0) + (
        pl.program_id(0) * row_count
    )
    lanes = lax.broadcasted_iota(jnp.int32, (key_count, 128), 1)

    def one_group(group, total):
        picked = chosen_ref[pl.ds(group, 1), :]
        hits = jnp.where(row_ids == picked, 1.0, 0.0).astype(jnp.bfloat16)
        place = jnp.where(lanes == group, 1.0, 0.0).astype(jnp.bfloat16)
        return total + project(hits, place)

    total = lax.fori_loop(0, group_count, one_group, jnp.zeros((row_count, 128), jnp.float32))
    out_ref[...] = jnp.where(total > 0.0, jnp.log2(jnp.maximum(total, 1.0)), masked_score)


def log_multiplicity(chosen, counts, table_rows):
    group_count, key_count = chosen.shape
    valid = jnp.arange(key_count, dtype=jnp.int32)[None, :] < counts[:, None]
    chosen = jnp.where(valid, chosen, -1)
    block = math.gcd(table_rows, 512)
    return pl.pallas_call(
        multiplicity_kernel,
        grid=(table_rows // block,),
        in_specs=[pl.BlockSpec((group_count, key_count), lambda i: (0, 0))],
        out_specs=pl.BlockSpec((block, 128), lambda i: (i, 0)),
        out_shape=jax.ShapeDtypeStruct((table_rows, 128), jnp.float32),
        name="multiplicity",
    )(chosen)


def fill_bias(counts_ref, bias_ref, span):
    row_count = bias_ref.shape[0]
    lanes = lax.broadcasted_iota(jnp.int32, (row_count, 128), 1)
    counts = counts_ref[...]
    for part in range(span):
        group = pl.program_id(0) * span + part
        column = jnp.sum(jnp.where(lanes == group, counts, 0.0), axis=1, keepdims=True)
        bias_ref[:, part * GROUP : (part + 1) * GROUP] = jnp.broadcast_to(
            column, (row_count, GROUP)
        )


def cross_forward_kernel(
    counts_ref, query_ref, key_ref, value_t_ref, out_ref, log_ref, bias_ref, *, heads, span, scale
):
    fill_bias(counts_ref, bias_ref, span)
    for head in range(heads):
        cols = slice(head * HEAD_DIM, (head + 1) * HEAD_DIM)
        scores = times_transposed(key_ref[:, cols], query_ref[:, cols])
        scores = scores * (scale * log2_e) + bias_ref[...]
        top = jnp.max(scores, axis=0, keepdims=True)
        raised = jnp.exp2(scores - top)
        total = jnp.sum(raised, axis=0, keepdims=True)
        mixed = project(value_t_ref[cols, :], raised.astype(jnp.bfloat16)) / total
        out_ref[:, cols] = mixed.T.astype(jnp.bfloat16)
        log_ref[0, head : head + 1, :] = top + jnp.log2(total)


def cross_forward(log_counts, queries, key_table, value_table_t, scale):
    row_count, width = queries.shape
    table_rows = key_table.shape[0]
    heads = width // HEAD_DIM
    groups = row_count // GROUP
    span = 2 if groups % 2 == 0 else 1
    rows = span * GROUP
    work = row_count * table_rows * width
    return pl.pallas_call(
        functools.partial(cross_forward_kernel, heads=heads, span=span, scale=scale),
        grid=(groups // span,),
        in_specs=[
            pl.BlockSpec((table_rows, 128), lambda i: (0, 0)),
            pl.BlockSpec((rows, width), lambda i: (i, 0)),
            pl.BlockSpec((table_rows, width), lambda i: (0, 0)),
            pl.BlockSpec((width, table_rows), lambda i: (0, 0)),
        ],
        out_specs=[
            pl.BlockSpec((rows, width), lambda i: (i, 0)),
            pl.BlockSpec((1, heads, rows), lambda i: (i, 0, 0)),
        ],
        out_shape=[
            jax.ShapeDtypeStruct((row_count, width), jnp.bfloat16),
            jax.ShapeDtypeStruct((groups // span, heads, rows), jnp.float32),
        ],
        scratch_shapes=[pltpu.VMEM((table_rows, rows), jnp.float32)],
        compiler_params=pltpu.CompilerParams(vmem_limit_bytes=vmem_bytes),
        cost_estimate=pl.CostEstimate(
            flops=8 * work, transcendentals=work // HEAD_DIM, bytes_accessed=4 * queries.size * 2
        ),
        name="cross_forward",
    )(log_counts, queries, key_table, value_table_t)


def cross_backward_kernel(
    counts_ref,
    query_ref,
    grad_ref,
    log_ref,
    key_ref,
    key_t_ref,
    value_ref,
    grad_query_ref,
    grad_key_ref,
    grad_value_ref,
    bias_ref,
    key_sum_ref,
    value_sum_ref,
    *,
    heads,
    span,
    scale,
):
    step = pl.program_id(0)

    @pl.when(step == 0)
    def _():
        key_sum_ref[...] = jnp.zeros_like(key_sum_ref)
        value_sum_ref[...] = jnp.zeros_like(value_sum_ref)

    fill_bias(counts_ref, bias_ref, span)
    for head in range(heads):
        cols = slice(head * HEAD_DIM, (head + 1) * HEAD_DIM)
        query = query_ref[:, cols]
        grad = grad_ref[:, cols]
        scores = times_transposed(key_ref[:, cols], query)
        weights = jnp.exp2(
            scores * (scale * log2_e) + bias_ref[...] - log_ref[0, head : head + 1, :]
        )
        grad_weights = times_transposed(value_ref[:, cols], grad)
        inner = jnp.sum(weights * grad_weights, axis=0, keepdims=True)
        grad_scores = (weights * (grad_weights - inner)).astype(jnp.bfloat16)
        value_sum_ref[:, cols] += project(weights.astype(jnp.bfloat16), grad)
        key_sum_ref[:, cols] += project(grad_scores, query)
        grad_query = project(key_t_ref[cols, :], grad_scores) * scale
        grad_query_ref[:, cols] = grad_query.T.astype(jnp.bfloat16)

    @pl.when(step == pl.num_programs(0) - 1)
    def _():
        grad_key_ref[...] = (key_sum_ref[...] * scale).astype(jnp.bfloat16)
        grad_value_ref[...] = value_sum_ref[...].astype(jnp.bfloat16)


def cross_backward(
    log_counts, queries, grad_attended, logs, key_table, key_table_t, value_table, scale
):
    row_count, width = queries.shape
    table_rows = key_table.shape[0]
    heads = width // HEAD_DIM
    groups = row_count // GROUP
    span = 2 if groups % 2 == 0 else 1
    rows = span * GROUP
    work = row_count * table_rows * width
    whole = pl.BlockSpec((table_rows, width), lambda i: (0, 0))
    block = pl.BlockSpec((rows, width), lambda i: (i, 0))
    return pl.pallas_call(
        functools.partial(cross_backward_kernel, heads=heads, span=span, scale=scale),
        grid=(groups // span,),
        in_specs=[
            pl.BlockSpec((table_rows, 128), lambda i: (0, 0)),
            block,
            block,
            pl.BlockSpec((1, heads, rows), lambda i: (i, 0, 0)),
            whole,
            pl.BlockSpec((width, table_rows), lambda i: (0, 0)),
            whole,
        ],
        out_specs=[block, whole, whole],
        out_shape=[
            jax.ShapeDtypeStruct((row_count, width), jnp.bfloat16),
            jax.ShapeDtypeStruct((table_rows, width), jnp.bfloat16),
            jax.ShapeDtypeStruct((table_rows, width), jnp.bfloat16),
        ],
        scratch_shapes=[
            pltpu.VMEM((table_rows, rows), jnp.float32),
            pltpu.VMEM((table_rows, width), jnp.float32),
            pltpu.VMEM((table_rows, width), jnp.float32),
        ],
        compiler_params=pltpu.CompilerParams(vmem_limit_bytes=vmem_bytes),
        cost_estimate=pl.CostEstimate(
            flops=20 * work, transcendentals=work // HEAD_DIM, bytes_accessed=8 * queries.size * 2
        ),
        name="cross_backward",
    )(log_counts, queries, grad_attended, logs, key_table, key_table_t, value_table)


def head_columns(head, heads_block):
    base = (head // heads_block) * 3 * heads_block + head % heads_block
    return [
        slice((base + kind * heads_block) * HEAD_DIM, (base + kind * heads_block + 1) * HEAD_DIM)
        for kind in range(3)
    ]


def self_forward_kernel(rows_ref, out_ref, log_ref, *, heads, heads_block, scale):
    for head in range(heads):
        query_cols, key_cols, value_cols = head_columns(head, heads_block)
        scores = times_transposed(rows_ref[:, key_cols], rows_ref[:, query_cols])
        scores = scores * (scale * log2_e)
        top = jnp.max(scores, axis=0, keepdims=True)
        raised = jnp.exp2(scores - top)
        total = jnp.sum(raised, axis=0, keepdims=True)
        weights = (raised / total).astype(jnp.bfloat16)
        mixed = transposed_times(weights, rows_ref[:, value_cols])
        out_ref[:, head * HEAD_DIM : (head + 1) * HEAD_DIM] = mixed.astype(jnp.bfloat16)
        log_ref[0, head : head + 1, :] = top + jnp.log2(total)


def self_forward(mixed_rows, heads, heads_block, scale):
    row_count, width = mixed_rows.shape
    groups = row_count // GROUP
    return pl.pallas_call(
        functools.partial(
            self_forward_kernel, heads=heads, heads_block=heads_block, scale=scale
        ),
        grid=(groups,),
        in_specs=[pl.BlockSpec((GROUP, width), lambda i: (i, 0))],
        out_specs=[
            pl.BlockSpec((GROUP, heads * HEAD_DIM), lambda i: (i, 0)),
            pl.BlockSpec((1, heads, GROUP), lambda i: (i, 0, 0)),
        ],
        out_shape=[
            jax.ShapeDtypeStruct((row_count, heads * HEAD_DIM), jnp.bfloat16),
            jax.ShapeDtypeStruct((groups, heads, GROUP), jnp.float32),
        ],
        cost_estimate=pl.CostEstimate(
            flops=8 * row_count * GROUP * heads * HEAD_DIM,
            transcendentals=row_count * GROUP * heads,
            bytes_accessed=3 * mixed_rows.size,
        ),
        name="self_forward",
    )(mixed_rows)


def self_backward_kernel(rows_ref, grad_ref, log_ref, out_ref, *, heads, heads_block, scale):
    for head in range(heads):
        query_cols, key_cols, value_cols = head_columns(head, heads_block)
        query = rows_ref[:, query_cols]
        key = rows_ref[:, key_cols]
        grad = grad_ref[:, head * HEAD_DIM : (head + 1) * HEAD_DIM]
        scores = times_transposed(key, query) * (scale * log2_e)
        weights = jnp.exp2(scores - log_ref[0, head : head + 1, :])
        grad_weights = times_transposed(rows_ref[:, value_cols], grad)
        inner = jnp.sum(weights * grad_weights, axis=0, keepdims=True)
        grad_scores = (weights * (grad_weights - inner)).astype(jnp.bfloat16)
        out_ref[:, value_cols] = project(weights.astype(jnp.bfloat16), grad).astype(jnp.bfloat16)
        out_ref[:, key_cols] = (project(grad_scores, query) * scale).astype(jnp.bfloat16)
        out_ref[:, query_cols] = (transposed_times(grad_scores, key) * scale).astype(jnp.bfloat16)


def self_backward(mixed_rows, grad_attended, logs, heads, heads_block, scale):
    row_count, width = mixed_rows.shape
    groups = row_count // GROUP
    return pl.pallas_call(
        functools.partial(
            self_backward_kernel, heads=heads, heads_block=heads_block, scale=scale
        ),
        grid=(groups,),
        in_specs=[
            pl.BlockSpec((GROUP, width), lambda i: (i, 0)),
            pl.BlockSpec((GROUP, heads * HEAD_DIM), lambda i: (i, 0)),
            pl.BlockSpec((1, heads, GROUP), lambda i: (i, 0, 0)),
        ],
        out_specs=pl.BlockSpec((GROUP, width), lambda i: (i, 0)),
        out_shape=jax.ShapeDtypeStruct((row_count, width), jnp.bfloat16),
        cost_estimate=pl.CostEstimate(
            flops=20 * row_count * GROUP * heads * HEAD_DIM,
            transcendentals=row_count * GROUP * heads,
            bytes_accessed=5 * mixed_rows.size,
        ),
        name="self_backward",
    )(mixed_rows, grad_attended, logs)


def feed_kernel(rows_ref, grad_ref, up_ref, down_ref, *rest):
    active_ref, grad_hidden_ref = rest[-2:]
    hidden = project(rows_ref[...], up_ref[...])
    grad_active = times_transposed(grad_ref[...], down_ref[...])
    square = hidden * hidden
    bend = jnp.tanh(gelu_factor * hidden * (1.0 + gelu_cubic * square))
    half_sum = 0.5 * (1.0 + bend)
    slope = half_sum + (0.5 * gelu_factor) * hidden * (1.0 - bend * bend) * (
        1.0 + (3.0 * gelu_cubic) * square
    )
    active_ref[...] = (hidden * half_sum).astype(jnp.bfloat16)
    grad_hidden_ref[...] = (slope * grad_active).astype(jnp.bfloat16)


def feed_block(step, total, rows, grads, up, down, earlier):
    row_count, width = rows.shape
    hidden_width = up.shape[1]
    tile = math.gcd(hidden_width, 256)
    result = jax.ShapeDtypeStruct((total * row_count, hidden_width), jnp.bfloat16)
    block = pl.BlockSpec((row_count, tile), lambda i: (step, i))
    whole = pl.BlockSpec((row_count, width), lambda i: (0, 0))
    return pl.pallas_call(
        feed_kernel,
        grid=(hidden_width // tile,),
        in_specs=[
            whole,
            whole,
            pl.BlockSpec((width, tile), lambda i: (0, i)),
            pl.BlockSpec((tile, width), lambda i: (i, 0)),
        ]
        + [pl.BlockSpec(memory_space=pl.ANY)] * len(earlier),
        out_specs=[block, block],
        out_shape=[result, result],
        input_output_aliases={4: 0, 5: 1} if earlier else {},
        compiler_params=pltpu.CompilerParams(vmem_limit_bytes=vmem_bytes),
        cost_estimate=pl.CostEstimate(
            flops=4 * row_count * width * hidden_width,
            transcendentals=row_count * hidden_width,
            bytes_accessed=4 * (width * hidden_width + row_count * (width + hidden_width)),
        ),
        name="feed_hidden",
    )(rows, grads, up, down, *earlier)


def local(
    latents,
    inputs,
    neighbours,
    key_counts,
    filled,
    cotangent,
    cross_gain,
    cross_query,
    cross_key,
    cross_value,
    cross_output,
    self_gain,
    self_query,
    self_key,
    self_value,
    self_output,
    feed_gain,
    feed_up,
    feed_down,
):
    tp_count = lax.axis_size("tp")
    tp_index = lax.axis_index("tp")
    bits = all_bits()
    rows_dev = latents.shape[0]
    table_dev = inputs.shape[0]
    table_rows = table_dev * tp_count
    group_count = neighbours.shape[0]
    local_groups = rows_dev // GROUP
    scale = 1.0 / math.sqrt(HEAD_DIM)
    first_group = tp_index * local_groups
    group_alive = (first_group + jnp.arange(local_groups, dtype=jnp.int32) < filled[0]).astype(
        jnp.float32
    )
    alive_rows = jnp.repeat(group_alive, GROUP)[:, None]

    chosen = jnp.roll(neighbours, -first_group, axis=0)
    counts = jnp.roll(key_counts, -first_group, axis=0)
    chosen = (chosen - tp_index * table_dev) % table_rows
    log_counts = log_multiplicity(chosen, counts, table_rows)

    def block_rows(array, step):
        return array[step * rows_dev : (step + 1) * rows_dev]

    state_rows = latents.astype(jnp.float32)
    unit_cross, inverse_cross, normed_cross = norm_forward(state_rows, cross_gain)
    embedded = jnp.concatenate(gather_blocks(inputs), axis=0)
    rows_cross = jnp.concatenate(gather_blocks(normed_cross), axis=0)
    key_table = project(embedded, cross_key).astype(jnp.bfloat16)
    value_table = project(embedded, cross_value).astype(jnp.bfloat16)
    key_table_t = key_table.T
    value_table_t = value_table.T
    queries_cross = project(rows_cross, cross_query).astype(jnp.bfloat16)
    attended_cross, logs_cross = cross_forward(
        log_counts, queries_cross, key_table, value_table_t, scale
    )
    after_cross = state_rows + alive_rows * sum_blocks(
        lambda step: project(block_rows(attended_cross, step), cross_output)
    )

    own_mixed = jnp.concatenate([self_query, self_key, self_value], axis=1)
    heads_block = self_query.shape[1] // HEAD_DIM
    heads = heads_block * tp_count

    def fetch(weight):
        kept, _ = halves(weight, 0)
        parts = [weight]
        for step in range(1, tp_count):
            part = from_peer(kept, step)
            parts.append(spread_sets(part, [0]))
        return parts

    mixed_weight = jnp.concatenate(fetch(own_mixed), axis=1)
    output_weight = jnp.concatenate(fetch(self_output), axis=0)

    unit_self, inverse_self, normed_self = norm_forward(after_cross, self_gain)
    mixed_rows = project(normed_self, mixed_weight).astype(jnp.bfloat16)
    attended_self, logs_self = self_forward(mixed_rows, heads, heads_block, scale)
    after_self = after_cross + alive_rows * project(attended_self, output_weight)

    grad_final = cotangent.astype(jnp.float32)
    grad_blocks = gather_blocks((alive_rows * grad_final).astype(jnp.bfloat16))
    unit_feed, inverse_feed, normed_feed = norm_forward(after_self, feed_gain)
    feed_blocks = gather_blocks(normed_feed)
    filled_parts = ()
    for step in range(tp_count):
        filled_parts = feed_block(
            step, tp_count, feed_blocks[step], grad_blocks[step], feed_up, feed_down, filled_parts
        )
    activated, grad_hidden = filled_parts
    grad_normed_feed = sum_blocks(
        lambda step: times_transposed(block_rows(grad_hidden, step), feed_up)
    )
    final_rows = after_self + alive_rows * sum_blocks(
        lambda step: project(block_rows(activated, step), feed_down)
    )
    grad_feed_up = transposed_times(jnp.concatenate(feed_blocks, axis=0), grad_hidden)
    grad_feed_down = transposed_times(activated, jnp.concatenate(grad_blocks, axis=0))
    grad_feed_up = sum_sets(grad_feed_up, bits)
    grad_feed_down = sum_sets(grad_feed_down, bits)
    group_rms = jnp.sqrt(jnp.mean((final_rows * final_rows).reshape(local_groups, -1), axis=1))
    penalty_term = jnp.sum(group_rms * group_alive)
    grad_rows, grad_feed_gain = norm_backward(grad_normed_feed, unit_feed, inverse_feed, feed_gain)
    grad_after_self = grad_final + grad_rows

    grad_branch = (alive_rows * grad_after_self).astype(jnp.bfloat16)
    grad_output_full = transposed_times(attended_self, grad_branch).astype(jnp.bfloat16)
    grad_attended = times_transposed(grad_branch, output_weight).astype(jnp.bfloat16)
    grad_mixed = self_backward(mixed_rows, grad_attended, logs_self, heads, heads_block, scale)
    grad_normed_self = times_transposed(grad_mixed, mixed_weight)
    grad_mixed_full = transposed_times(normed_self, grad_mixed).astype(jnp.bfloat16)
    grad_rows, grad_self_gain = norm_backward(grad_normed_self, unit_self, inverse_self, self_gain)
    grad_after_cross = grad_after_self + grad_rows

    def own_share(parts):
        shares = [scatter_sets(part, bits[:1]) for part in parts]
        total = shares[0].astype(jnp.float32)
        for step in range(1, tp_count):
            total = total + to_peer(shares[step], step).astype(jnp.float32)
        part = scatter_sets(total.astype(jnp.bfloat16), bits[1:])
        return spread_sets(part, bits).astype(jnp.float32)

    grad_self_mixed = own_share(jnp.split(grad_mixed_full, tp_count, axis=1))
    grad_self_output = own_share(jnp.split(grad_output_full, tp_count, axis=0))
    grad_self_query, grad_self_key, grad_self_value = jnp.split(grad_self_mixed, 3, axis=1)

    grad_branch = jnp.concatenate(
        gather_blocks((alive_rows * grad_after_cross).astype(jnp.bfloat16)), axis=0
    )
    grad_cross_output = sum_sets(transposed_times(attended_cross, grad_branch), bits)
    grad_attended = times_transposed(grad_branch, cross_output).astype(jnp.bfloat16)
    grad_queries, grad_key_table, grad_value_table = cross_backward(
        log_counts,
        queries_cross,
        grad_attended,
        logs_cross,
        key_table,
        key_table_t,
        value_table,
        scale,
    )
    grad_cross_mixed = jnp.concatenate(
        [
            transposed_times(rows_cross, grad_queries).astype(jnp.bfloat16),
            transposed_times(embedded, grad_key_table).astype(jnp.bfloat16),
            transposed_times(embedded, grad_value_table).astype(jnp.bfloat16),
        ],
        axis=1,
    )
    grad_cross_mixed = sum_sets(grad_cross_mixed, bits)
    grad_cross_query, grad_cross_key, grad_cross_value = jnp.split(grad_cross_mixed, 3, axis=1)
    input_grad = sum_blocks(
        lambda step: times_transposed(
            grad_key_table[step * table_dev : (step + 1) * table_dev], cross_key
        )
        + times_transposed(
            grad_value_table[step * table_dev : (step + 1) * table_dev], cross_value
        )
    )
    grad_normed_cross = sum_blocks(
        lambda step: times_transposed(block_rows(grad_queries, step), cross_query)
    )
    grad_rows, grad_cross_gain = norm_backward(
        grad_normed_cross, unit_cross, inverse_cross, cross_gain
    )
    latent_grad = grad_after_cross + grad_rows

    early = jnp.stack(
        [grad_feed_gain, grad_self_gain, jnp.full_like(grad_feed_gain, penalty_term)], axis=0
    )
    early = sum_everywhere(early)
    grad_cross_gain = sum_everywhere(grad_cross_gain[None])[0]
    penalty = early[2, 0] / (group_count * lax.axis_size("sets"))
    return (
        final_rows.astype(jnp.bfloat16),
        latent_grad,
        input_grad,
        grad_cross_gain,
        grad_cross_query,
        grad_cross_key,
        grad_cross_value,
        grad_cross_output,
        early[1],
        grad_self_query,
        grad_self_key,
        grad_self_value,
        grad_self_output,
        early[0],
        grad_feed_up,
        grad_feed_down,
        penalty,
    )


def solution(mesh):
    return jax.shard_map(
        local,
        mesh=mesh,
        in_specs=(
            P(("sets", "tp"), None),
            P(("sets", "tp"), None),
            P("sets", None),
            P("sets"),
            P("sets"),
            P(("sets", "tp"), None),
            P(),
            P(None, "tp"),
            P(None, "tp"),
            P(None, "tp"),
            P("tp", None),
            P(),
            P(None, "tp"),
            P(None, "tp"),
            P(None, "tp"),
            P("tp", None),
            P(),
            P(None, "tp"),
            P("tp", None),
        ),
        out_specs=(
            P(("sets", "tp"), None),
            P(("sets", "tp"), None),
            P(("sets", "tp"), None),
            P(),
            P(None, "tp"),
            P(None, "tp"),
            P(None, "tp"),
            P("tp", None),
            P(),
            P(None, "tp"),
            P(None, "tp"),
            P(None, "tp"),
            P("tp", None),
            P(),
            P(None, "tp"),
            P("tp", None),
            P(),
        ),
        check_vma=False,
    )
```

```python
import functools
import math

import jax
import jax.numpy as jnp
from jax import lax
from jax.experimental import pallas as pl
from jax.experimental.pallas import tpu as pltpu
from jax.sharding import PartitionSpec as P

HEAD_DIM = 128
GROUP = 128

epsilon = 1e-05
masked_score = -1e30
gelu_factor = 0.7978845608028654
gelu_cubic = 0.044715
log2_e = 1.4426950408889634
vmem_bytes = 60 * 1024 * 1024
small_cost = pl.CostEstimate(flops=1000000, transcendentals=1000, bytes_accessed=100000)


def project(left_rows, right_rows):
    return jnp.dot(left_rows, right_rows, preferred_element_type=jnp.float32)


def times_transposed(left_rows, right_rows):
    return lax.dot_general(
        left_rows, right_rows, (((1,), (1,)), ((), ())), preferred_element_type=jnp.float32
    )


def transposed_times(left_rows, right_rows):
    return lax.dot_general(
        left_rows, right_rows, (((0,), (0,)), ((), ())), preferred_element_type=jnp.float32
    )


def norm_forward(values, gain):
    average = jnp.mean(values, axis=1, keepdims=True)
    centred = values - average
    variance = jnp.mean(centred * centred, axis=1, keepdims=True)
    inverse = lax.rsqrt(variance + epsilon)
    unit_rows = centred * inverse
    return (unit_rows, inverse, (unit_rows * gain).astype(jnp.bfloat16))


def norm_backward(grad_normed, unit_rows, inverse, gain):
    scaled = grad_normed * gain
    first_mean = jnp.mean(scaled, axis=1, keepdims=True)
    second_mean = jnp.mean(scaled * unit_rows, axis=1, keepdims=True)
    grad_rows = inverse * (scaled - first_mean - unit_rows * second_mean)
    return (grad_rows, jnp.sum(grad_normed * unit_rows, axis=0))


def from_peer(block, step):
    count = lax.axis_size("tp")
    return lax.ppermute(block, "tp", [(source, (source - step) % count) for source in range(count)])


def to_peer(block, step):
    count = lax.axis_size("tp")
    return lax.ppermute(block, "tp", [(source, (source + step) % count) for source in range(count)])


def gather_blocks(block):
    return [block] + [from_peer(block, step) for step in range(1, lax.axis_size("tp"))]


def sum_blocks(make_partial):
    received = [
        to_peer(make_partial(step).astype(jnp.bfloat16), step)
        for step in range(1, lax.axis_size("tp"))
    ]
    total = make_partial(0)
    for term in received:
        total = total + term.astype(jnp.float32)
    return total


def swap_sets(block, bit):
    count = lax.axis_size("sets")
    return lax.ppermute(block, "sets", [(source, source ^ (1 << bit)) for source in range(count)])


def set_bit(bit):
    return (lax.axis_index("sets") >> bit) & 1


def halves(block, bit, before=0):
    rows, columns = block.shape[-2:]
    lead = block.shape[:-2]
    view = block.reshape(lead + (2**before, 2, rows // 2 ** (before + 1), columns))
    axis = view.ndim - 3
    mine = set_bit(bit)
    kept, sent = [
        lax.dynamic_slice_in_dim(view, place, 1, axis).reshape(lead + (rows // 2, columns))
        for place in (mine, 1 - mine)
    ]
    return (kept, sent)


def add_pair(kept, received):
    return (kept.astype(jnp.float32) + received.astype(jnp.float32)).astype(jnp.bfloat16)


class Order:
    def __init__(self):
        self.last = ()

    def hold(self, value):
        if not self.last:
            return value
        return lax.optimization_barrier((value, *self.last))[0]

    def mark(self, *values):
        self.last = values


def join(block, received, bit):
    first = set_bit(bit) == 0
    return jnp.concatenate(
        [jnp.where(first, block, received), jnp.where(first, received, block)],
        axis=block.ndim - 2,
    )


def all_bits():
    return list(range(int(math.log2(lax.axis_size("sets")))))


class SetSum:
    def __init__(self, order, block, halve, layout=None, peers_after=None, double=True):
        self.order = order
        self.block = block.astype(jnp.bfloat16)
        self.layout = list(halve if layout is None else layout)
        self.stages = [("halve", bit) for bit in halve]
        if peers_after is not None:
            self.stages.insert(peers_after, ("peers", None))
        if double:
            self.stages += [("double", bit) for bit in reversed(halve)]
        self.last = None
        self.send()

    def send(self):
        kind, bit = self.stages[0]
        if kind == "halve":
            before = self.layout.index(bit)
            self.layout.remove(bit)
            self.kept, sent = halves(self.block, bit, before)
            self.received = [swap_sets(sent, bit)]
        elif kind == "peers":
            self.kept, sent = self.block[0], self.block[1:]
            self.received = [
                to_peer(sent[step], step + 1) for step in range(sent.shape[0])
            ]
        else:
            self.kept = sent = self.block
            self.received = [swap_sets(sent, bit)]
        self.order.mark(sent)

    def advance(self):
        if not self.stages:
            return
        kind, bit = self.stages.pop(0)
        received = self.order.hold(tuple(self.received))
        if kind == "double" and not self.stages:
            self.last = (self.kept, received[0], bit)
            self.order.mark(received[0])
            return
        if kind == "double":
            self.block = join(self.kept, received[0], bit)
        else:
            total = self.kept.astype(jnp.float32)
            for term in received:
                total = total + term.astype(jnp.float32)
            self.block = total.astype(jnp.bfloat16)
        if self.stages:
            self.send()
        else:
            self.order.mark(self.block)

    def result(self, place=None):
        kept, received, bit = self.last
        if place is not None:
            kept, received = kept[place], received[place]
        return join(kept, received, bit).astype(jnp.float32)


def stack_output(weight):
    width = weight.shape[0]
    return jnp.concatenate(
        [weight[:, start : start + width] for start in range(0, weight.shape[1], width)], axis=0
    )


def unstack_output(stacked):
    width = stacked.shape[1]
    return jnp.concatenate(
        [stacked[start : start + width] for start in range(0, stacked.shape[0], width)], axis=1
    )


def multiplicity_kernel(chosen_ref, out_ref):
    row_count = out_ref.shape[0]
    group_count, key_count = chosen_ref.shape
    row_ids = lax.broadcasted_iota(jnp.int32, (row_count, key_count), 0) + (
        pl.program_id(0) * row_count
    )
    lanes = lax.broadcasted_iota(jnp.int32, (key_count, 128), 1)

    def one_group(group, total):
        picked = chosen_ref[pl.ds(group, 1), :]
        hits = jnp.where(row_ids == picked, 1.0, 0.0).astype(jnp.bfloat16)
        place = jnp.where(lanes == group, 1.0, 0.0).astype(jnp.bfloat16)
        return total + project(hits, place)

    total = lax.fori_loop(0, group_count, one_group, jnp.zeros((row_count, 128), jnp.float32))
    out_ref[...] = jnp.where(total > 0.0, jnp.log2(jnp.maximum(total, 1.0)), masked_score)


def log_multiplicity(chosen, counts, table_rows):
    group_count, key_count = chosen.shape
    valid = jnp.arange(key_count, dtype=jnp.int32)[None, :] < counts[:, None]
    chosen = jnp.where(valid, chosen, -1)
    block = math.gcd(table_rows, 512)
    return pl.pallas_call(
        multiplicity_kernel,
        grid=(table_rows // block,),
        in_specs=[pl.BlockSpec((group_count, key_count), lambda i: (0, 0))],
        out_specs=pl.BlockSpec((block, 128), lambda i: (i, 0)),
        out_shape=jax.ShapeDtypeStruct((table_rows, 128), jnp.float32),
        name="multiplicity",
    )(chosen)


def fill_bias(counts_ref, bias_ref, span, first_group):
    row_count = bias_ref.shape[0]
    lanes = lax.broadcasted_iota(jnp.int32, (row_count, 128), 1)
    counts = counts_ref[...]
    for part in range(span):
        group = first_group + pl.program_id(0) * span + part
        column = jnp.sum(jnp.where(lanes == group, counts, 0.0), axis=1, keepdims=True)
        bias_ref[:, part * GROUP : (part + 1) * GROUP] = jnp.broadcast_to(
            column, (row_count, GROUP)
        )


def cross_forward_kernel(
    counts_ref,
    query_ref,
    key_ref,
    value_t_ref,
    out_ref,
    log_ref,
    bias_ref,
    *,
    heads,
    span,
    scale,
    first_group,
):
    fill_bias(counts_ref, bias_ref, span, first_group)
    for head in range(heads):
        cols = slice(head * HEAD_DIM, (head + 1) * HEAD_DIM)
        scores = times_transposed(key_ref[:, cols], query_ref[:, cols])
        scores = scores * (scale * log2_e) + bias_ref[...]
        top = jnp.max(scores, axis=0, keepdims=True)
        raised = jnp.exp2(scores - top)
        total = jnp.sum(raised, axis=0, keepdims=True)
        mixed = project(value_t_ref[cols, :], raised.astype(jnp.bfloat16)) / total
        out_ref[:, cols] = mixed.T.astype(jnp.bfloat16)
        log_ref[0, head : head + 1, :] = top + jnp.log2(total)


def cross_forward(log_counts, queries, key_table, value_table_t, scale, first_group):
    row_count, width = queries.shape
    table_rows = key_table.shape[0]
    heads = width // HEAD_DIM
    groups = row_count // GROUP
    span = 2 if groups % 2 == 0 else 1
    rows = span * GROUP
    return pl.pallas_call(
        functools.partial(
            cross_forward_kernel, heads=heads, span=span, scale=scale, first_group=first_group
        ),
        grid=(groups // span,),
        in_specs=[
            pl.BlockSpec((table_rows, 128), lambda i: (0, 0)),
            pl.BlockSpec((rows, width), lambda i: (i, 0)),
            pl.BlockSpec((table_rows, width), lambda i: (0, 0)),
            pl.BlockSpec((width, table_rows), lambda i: (0, 0)),
        ],
        out_specs=[
            pl.BlockSpec((rows, width), lambda i: (i, 0)),
            pl.BlockSpec((1, heads, rows), lambda i: (i, 0, 0)),
        ],
        out_shape=[
            jax.ShapeDtypeStruct((row_count, width), jnp.bfloat16),
            jax.ShapeDtypeStruct((groups // span, heads, rows), jnp.float32),
        ],
        scratch_shapes=[pltpu.VMEM((table_rows, rows), jnp.float32)],
        compiler_params=pltpu.CompilerParams(vmem_limit_bytes=vmem_bytes),
        cost_estimate=small_cost,
        name="cross_forward",
    )(log_counts, queries, key_table, value_table_t)


def cross_backward_kernel(*refs, heads, span, scale, first_group, start, finish):
    counts_ref, query_ref, grad_ref, log_ref, key_ref, key_t_ref, value_ref = refs[:7]
    refs = refs[7:]
    if not start:
        key_start_ref, value_start_ref = refs[:2]
        refs = refs[2:]
    grad_query_ref, grad_key_ref, grad_value_ref, bias_ref = refs[:4]
    key_sum_ref, value_sum_ref = refs[4:] if finish else (grad_key_ref, grad_value_ref)
    step = pl.program_id(0)

    @pl.when(step == 0)
    def _():
        if start:
            key_sum_ref[...] = jnp.zeros_like(key_sum_ref)
            value_sum_ref[...] = jnp.zeros_like(value_sum_ref)
        else:
            key_sum_ref[...] = key_start_ref[...]
            value_sum_ref[...] = value_start_ref[...]

    fill_bias(counts_ref, bias_ref, span, first_group)
    for head in range(heads):
        cols = slice(head * HEAD_DIM, (head + 1) * HEAD_DIM)
        query = query_ref[:, cols]
        grad = grad_ref[:, cols]
        scores = times_transposed(key_ref[:, cols], query)
        weights = jnp.exp2(
            scores * (scale * log2_e) + bias_ref[...] - log_ref[0, head : head + 1, :]
        )
        grad_weights = times_transposed(value_ref[:, cols], grad)
        inner = jnp.sum(weights * grad_weights, axis=0, keepdims=True)
        grad_scores = (weights * (grad_weights - inner)).astype(jnp.bfloat16)
        value_sum_ref[:, cols] += project(weights.astype(jnp.bfloat16), grad)
        key_sum_ref[:, cols] += project(grad_scores, query)
        grad_query = project(key_t_ref[cols, :], grad_scores) * scale
        grad_query_ref[:, cols] = grad_query.T.astype(jnp.bfloat16)

    if finish:

        @pl.when(step == pl.num_programs(0) - 1)
        def _():
            grad_key_ref[...] = (key_sum_ref[...] * scale).astype(jnp.bfloat16)
            grad_value_ref[...] = value_sum_ref[...].astype(jnp.bfloat16)


def cross_backward(
    log_counts,
    queries,
    grad_attended,
    logs,
    key_table,
    key_table_t,
    value_table,
    scale,
    first_group,
    earlier,
    finish,
):
    row_count, width = queries.shape
    table_rows = key_table.shape[0]
    heads = width // HEAD_DIM
    groups = row_count // GROUP
    span = 2 if groups % 2 == 0 else 1
    rows = span * GROUP
    whole = pl.BlockSpec((table_rows, width), lambda i: (0, 0))
    block = pl.BlockSpec((rows, width), lambda i: (i, 0))
    table_type = jnp.bfloat16 if finish else jnp.float32
    sums = pltpu.VMEM((table_rows, width), jnp.float32)
    return pl.pallas_call(
        functools.partial(
            cross_backward_kernel,
            heads=heads,
            span=span,
            scale=scale,
            first_group=first_group,
            start=not earlier,
            finish=finish,
        ),
        grid=(groups // span,),
        in_specs=[
            pl.BlockSpec((table_rows, 128), lambda i: (0, 0)),
            block,
            block,
            pl.BlockSpec((1, heads, rows), lambda i: (i, 0, 0)),
            whole,
            pl.BlockSpec((width, table_rows), lambda i: (0, 0)),
            whole,
        ]
        + [whole] * len(earlier),
        out_specs=[block, whole, whole],
        out_shape=[
            jax.ShapeDtypeStruct((row_count, width), jnp.bfloat16),
            jax.ShapeDtypeStruct((table_rows, width), table_type),
            jax.ShapeDtypeStruct((table_rows, width), table_type),
        ],
        scratch_shapes=[pltpu.VMEM((table_rows, rows), jnp.float32)]
        + ([sums, sums] if finish else []),
        compiler_params=pltpu.CompilerParams(vmem_limit_bytes=vmem_bytes),
        cost_estimate=small_cost,
        name="cross_backward",
    )(log_counts, queries, grad_attended, logs, key_table, key_table_t, value_table, *earlier)


def head_columns(head, heads_block):
    base = (head // heads_block) * 3 * heads_block + head % heads_block
    return [
        slice((base + kind * heads_block) * HEAD_DIM, (base + kind * heads_block + 1) * HEAD_DIM)
        for kind in range(3)
    ]


def self_forward_kernel(rows_ref, out_ref, log_ref, *, heads, heads_block, scale):
    columns = [head_columns(head, heads_block) for head in range(heads)]
    scores = [
        times_transposed(rows_ref[:, key_cols], rows_ref[:, query_cols])
        for query_cols, key_cols, _ in columns
    ]
    weights = []
    for head in range(heads):
        scaled = scores[head] * (scale * log2_e)
        top = jnp.max(scaled, axis=0, keepdims=True)
        raised = jnp.exp2(scaled - top)
        total = jnp.sum(raised, axis=0, keepdims=True)
        weights.append((raised * (1.0 / total)).astype(jnp.bfloat16))
        log_ref[0, head : head + 1, :] = top + jnp.log2(total)
    for head in range(heads):
        mixed = transposed_times(weights[head], rows_ref[:, columns[head][2]])
        out_ref[:, head * HEAD_DIM : (head + 1) * HEAD_DIM] = mixed.astype(jnp.bfloat16)


def self_forward(mixed_rows, heads, heads_block, scale):
    row_count, width = mixed_rows.shape
    groups = row_count // GROUP
    return pl.pallas_call(
        functools.partial(
            self_forward_kernel, heads=heads, heads_block=heads_block, scale=scale
        ),
        grid=(groups,),
        in_specs=[pl.BlockSpec((GROUP, width), lambda i: (i, 0))],
        out_specs=[
            pl.BlockSpec((GROUP, heads * HEAD_DIM), lambda i: (i, 0)),
            pl.BlockSpec((1, heads, GROUP), lambda i: (i, 0, 0)),
        ],
        out_shape=[
            jax.ShapeDtypeStruct((row_count, heads * HEAD_DIM), jnp.bfloat16),
            jax.ShapeDtypeStruct((groups, heads, GROUP), jnp.float32),
        ],
        cost_estimate=small_cost,
        name="self_forward",
    )(mixed_rows)


def self_backward_kernel(rows_ref, grad_ref, log_ref, out_ref, *, heads, heads_block, scale):
    columns = [head_columns(head, heads_block) for head in range(heads)]
    grads = [slice(head * HEAD_DIM, (head + 1) * HEAD_DIM) for head in range(heads)]
    scores = [
        times_transposed(rows_ref[:, key_cols], rows_ref[:, query_cols])
        for query_cols, key_cols, _ in columns
    ]
    grad_weights = [
        times_transposed(rows_ref[:, columns[head][2]], grad_ref[:, grads[head]])
        for head in range(heads)
    ]
    weights, grad_scores = [], []
    for head in range(heads):
        soft = jnp.exp2(scores[head] * (scale * log2_e) - log_ref[0, head : head + 1, :])
        inner = jnp.sum(soft * grad_weights[head], axis=0, keepdims=True)
        grad_scores.append((soft * (grad_weights[head] - inner)).astype(jnp.bfloat16))
        weights.append(soft.astype(jnp.bfloat16))
    for head in range(heads):
        query_cols, key_cols, value_cols = columns[head]
        out_ref[:, value_cols] = project(weights[head], grad_ref[:, grads[head]]).astype(
            jnp.bfloat16
        )
        out_ref[:, key_cols] = (project(grad_scores[head], rows_ref[:, query_cols]) * scale).astype(
            jnp.bfloat16
        )
        out_ref[:, query_cols] = (
            transposed_times(grad_scores[head], rows_ref[:, key_cols]) * scale
        ).astype(jnp.bfloat16)


def self_backward(mixed_rows, grad_attended, logs, heads, heads_block, scale):
    row_count, width = mixed_rows.shape
    groups = row_count // GROUP
    return pl.pallas_call(
        functools.partial(
            self_backward_kernel, heads=heads, heads_block=heads_block, scale=scale
        ),
        grid=(groups,),
        in_specs=[
            pl.BlockSpec((GROUP, width), lambda i: (i, 0)),
            pl.BlockSpec((GROUP, heads * HEAD_DIM), lambda i: (i, 0)),
            pl.BlockSpec((1, heads, GROUP), lambda i: (i, 0, 0)),
        ],
        out_specs=pl.BlockSpec((GROUP, width), lambda i: (i, 0)),
        out_shape=jax.ShapeDtypeStruct((row_count, width), jnp.bfloat16),
        cost_estimate=small_cost,
        name="self_backward",
    )(mixed_rows, grad_attended, logs)


def feed_kernel(rows_ref, grad_ref, up_ref, down_ref, *rest):
    active_ref, grad_hidden_ref, grad_rows_ref, sum_ref = rest[-4:]
    step = pl.program_id(0)

    @pl.when(step == 0)
    def _():
        sum_ref[...] = jnp.zeros_like(sum_ref)

    hidden = project(rows_ref[...], up_ref[...])
    grad_active = times_transposed(grad_ref[...], down_ref[...])
    square = hidden * hidden
    bend = jnp.tanh(gelu_factor * hidden * (1.0 + gelu_cubic * square))
    half_sum = 0.5 * (1.0 + bend)
    slope = half_sum + (0.5 * gelu_factor) * hidden * (1.0 - bend * bend) * (
        1.0 + (3.0 * gelu_cubic) * square
    )
    grad_hidden = (slope * grad_active).astype(jnp.bfloat16)
    active_ref[...] = (hidden * half_sum).astype(jnp.bfloat16)
    grad_hidden_ref[...] = grad_hidden
    sum_ref[...] += times_transposed(grad_hidden, up_ref[...])

    @pl.when(step == pl.num_programs(0) - 1)
    def _():
        grad_rows_ref[...] = sum_ref[...].astype(grad_rows_ref.dtype)


def feed_block(first_row, total_rows, rows, grads, up, down, earlier, sum_type):
    row_count, width = rows.shape
    hidden_width = up.shape[1]
    tile = math.gcd(hidden_width, 512)
    place = first_row // row_count
    result = jax.ShapeDtypeStruct((total_rows, hidden_width), jnp.bfloat16)
    block = pl.BlockSpec((row_count, tile), lambda i: (place, i))
    whole = pl.BlockSpec((row_count, width), lambda i: (0, 0))
    return pl.pallas_call(
        feed_kernel,
        grid=(hidden_width // tile,),
        in_specs=[
            whole,
            whole,
            pl.BlockSpec((width, tile), lambda i: (0, i)),
            pl.BlockSpec((tile, width), lambda i: (i, 0)),
        ]
        + [pl.BlockSpec(memory_space=pl.ANY)] * len(earlier),
        out_specs=[block, block, whole],
        out_shape=[result, result, jax.ShapeDtypeStruct((row_count, width), sum_type)],
        scratch_shapes=[pltpu.VMEM((row_count, width), jnp.float32)],
        input_output_aliases={4: 0, 5: 1} if earlier else {},
        compiler_params=pltpu.CompilerParams(vmem_limit_bytes=vmem_bytes),
        cost_estimate=small_cost,
        name="feed_hidden",
    )(rows, grads, up, down, *earlier)


def local(
    latents,
    inputs,
    neighbours,
    key_counts,
    filled,
    cotangent,
    cross_gain,
    cross_query,
    cross_key,
    cross_value,
    cross_output,
    self_gain,
    self_query,
    self_key,
    self_value,
    self_output,
    feed_gain,
    feed_up,
    feed_down,
):
    tp_count = lax.axis_size("tp")
    tp_index = lax.axis_index("tp")
    bits = all_bits()
    rows_dev = latents.shape[0]
    table_dev = inputs.shape[0]
    table_rows = table_dev * tp_count
    group_count = neighbours.shape[0]
    local_groups = rows_dev // GROUP
    scale = 1.0 / math.sqrt(HEAD_DIM)
    first_group = tp_index * local_groups
    group_alive = (first_group + jnp.arange(local_groups, dtype=jnp.int32) < filled[0]).astype(
        jnp.float32
    )
    alive_rows = jnp.repeat(group_alive, GROUP)[:, None]

    chosen = jnp.roll(neighbours, -first_group, axis=0)
    counts = jnp.roll(key_counts, -first_group, axis=0)
    chosen = (chosen - tp_index * table_dev) % table_rows
    log_counts = log_multiplicity(chosen, counts, table_rows)

    def block_rows(array, step):
        return array[step * rows_dev : (step + 1) * rows_dev]

    def table_part(array, step):
        return array[step * table_dev : (step + 1) * table_dev]

    heads_block = self_query.shape[1] // HEAD_DIM
    heads = heads_block * tp_count
    width = heads_block * HEAD_DIM
    model = self_query.shape[0]
    hidden_width = feed_up.shape[1]
    feed_width = min(hidden_width, model)
    cross_first = bits[:1] + bits[2:] + bits[1:2]
    natural = list(reversed(bits))
    order = Order()

    piece_rows = rows_dev // 2 if local_groups % 2 == 0 else rows_dev
    piece_starts = list(range(0, rows_dev, piece_rows))

    def pieces(block):
        return [block[start : start + piece_rows] for start in piece_starts]

    peer_inputs = gather_blocks(inputs)
    own_slice = jnp.stack([self_query, self_key, self_value, stack_output(self_output)], axis=0)
    share = model // lax.axis_size("sets")
    own_slice = lax.dynamic_slice_in_dim(own_slice, lax.axis_index("sets") * share, share, 1)
    peer_slices = [from_peer(own_slice, step) for step in range(1, tp_count)]

    state_rows = latents.astype(jnp.float32)
    grad_final = cotangent.astype(jnp.float32)
    grad_own = (alive_rows * grad_final).astype(jnp.bfloat16)
    unit_cross, inverse_cross, normed_cross = norm_forward(state_rows, cross_gain)
    order.mark(normed_cross)
    log_counts = log_multiplicity(order.hold(chosen), counts, table_rows)
    order.mark(log_counts)
    embedded = jnp.concatenate(order.hold(tuple(peer_inputs)), axis=0)
    order.mark(embedded)
    rows_cross = gather_blocks(order.hold(normed_cross))
    peer_stacks = [
        lax.all_gather(part, "sets", axis=1, tiled=True) for part in order.hold(tuple(peer_slices))
    ]
    key_table = project(order.hold(embedded), cross_key).astype(jnp.bfloat16)
    value_table_t = lax.dot_general(
        cross_value, embedded, (((0,), (1,)), ((), ())), preferred_element_type=jnp.float32
    ).astype(jnp.bfloat16)
    order.mark(key_table, value_table_t)
    grad_pieces = [[] for _ in range(tp_count)]
    queries_cross, attended_cross, logs_cross = [], [], []
    for step in range(tp_count):
        queries = project(order.hold(rows_cross[step]), cross_query).astype(jnp.bfloat16)
        order.mark(queries)
        if step == tp_count - 1:
            for peer in range(1, tp_count):
                grad_pieces[peer].append(from_peer(order.hold(pieces(grad_own)[0]), peer))
        attended, logs = cross_forward(
            log_counts, order.hold(queries), key_table, value_table_t, scale, step * local_groups
        )
        order.mark(attended)
        queries_cross.append(queries)
        attended_cross.append(attended)
        logs_cross.append(logs)
    cross_terms = []
    for step in range(1, tp_count):
        grad_pieces[step][0] = order.hold(grad_pieces[step][0])
        term = project(attended_cross[step], cross_output).astype(jnp.bfloat16)
        cross_terms.append(to_peer(term, step))
        order.mark(term, grad_pieces[step][0])
    branch = project(order.hold(attended_cross[0]), cross_output)
    order.mark(branch)
    key_table_t = lax.dot_general(
        cross_key, order.hold(embedded), (((0,), (1,)), ((), ())), preferred_element_type=jnp.float32
    ).astype(jnp.bfloat16)
    value_table = project(order.hold(embedded), cross_value).astype(jnp.bfloat16)
    order.mark(key_table_t, value_table)
    peer_stacks = order.hold(tuple(peer_stacks))
    mixed_weight = jnp.concatenate(
        [self_query, self_key, self_value]
        + [stack[kind] for stack in peer_stacks for kind in range(3)],
        axis=1,
    )
    output_weight = jnp.concatenate(
        [self_output] + [unstack_output(stack[3]) for stack in peer_stacks], axis=0
    )
    mixed_weight, output_weight = lax.optimization_barrier((mixed_weight, output_weight))
    order.mark(mixed_weight, output_weight)
    for term in order.hold(tuple(cross_terms)):
        branch = branch + term.astype(jnp.float32)
    after_cross = state_rows + alive_rows * branch
    order.mark(after_cross)

    for piece in pieces(grad_own)[1:]:
        for step in range(1, tp_count):
            grad_pieces[step].append(from_peer(order.hold(piece), step))
    unit_self, inverse_self, normed_self = norm_forward(after_cross, self_gain)
    mixed_rows = project(normed_self, mixed_weight).astype(jnp.bfloat16)
    attended_self, logs_self = self_forward(mixed_rows, heads, heads_block, scale)
    order.mark(attended_self)
    for step in range(1, tp_count):
        grad_pieces[step] = list(order.hold(tuple(grad_pieces[step])))
    order.mark(attended_self, *[part for parts in grad_pieces for part in parts])
    after_self = after_cross + alive_rows * project(order.hold(attended_self), output_weight)

    unit_feed, inverse_feed, normed_feed = norm_forward(after_self, feed_gain)
    order.mark(normed_feed)
    feed_pieces = [[] for _ in range(tp_count)]
    for piece in pieces(normed_feed):
        for step in range(1, tp_count):
            feed_pieces[step].append(from_peer(piece, step))
    *filled_parts, grad_normed_feed = feed_block(
        0,
        rows_dev * tp_count,
        order.hold(normed_feed),
        grad_own,
        feed_up,
        feed_down,
        (),
        jnp.float32,
    )
    order.mark(*filled_parts)
    normed_terms = [[] for _ in range(tp_count)]
    for step in range(1, tp_count):
        for place, start in enumerate(piece_starts):
            *filled_parts, term = feed_block(
                step * rows_dev + start,
                rows_dev * tp_count,
                order.hold(feed_pieces[step][place]),
                grad_pieces[step][place],
                feed_up,
                feed_down,
                filled_parts,
                jnp.bfloat16,
            )
            normed_terms[step].append(to_peer(term, step))
            order.mark(term)
    activated, grad_hidden = filled_parts
    feed_all = jnp.concatenate(
        [normed_feed] + [piece for parts in feed_pieces for piece in parts], axis=0
    )
    grad_all = jnp.concatenate(
        [grad_own] + [piece for parts in grad_pieces for piece in parts], axis=0
    )
    received = [[] for _ in range(tp_count)]
    for place in range(len(piece_starts)):
        terms = order.hold(tuple(normed_terms[step][place] for step in range(1, tp_count)))
        for step in range(1, tp_count):
            received[step].append(terms[step - 1])
        order.mark(*terms)
        if place == 0:
            held = order.hold(grad_hidden)
            grad_up = jnp.stack(
                [
                    transposed_times(feed_all, held[:, start : start + feed_width])
                    for start in range(0, hidden_width, feed_width)
                ]
            )
            up_sum = SetSum(order, grad_up, bits, layout=natural, double=False)
    grad_down = transposed_times(order.hold(activated), grad_all).astype(jnp.bfloat16)
    if hidden_width >= model:
        grad_down = grad_down.reshape(hidden_width // model, model, model)
    else:
        grad_down = stack_output(grad_down)[None]
    down_sum = SetSum(order, grad_down, cross_first, layout=natural, double=False)
    up_sum.advance()
    for step in range(1, tp_count):
        term = jnp.concatenate(received[step], axis=0)
        grad_normed_feed = order.hold(grad_normed_feed) + term.astype(jnp.float32)
    order.mark(grad_normed_feed)
    grad_rows, grad_feed_gain = norm_backward(
        order.hold(grad_normed_feed), unit_feed, inverse_feed, feed_gain
    )
    grad_after_self = grad_final + grad_rows

    grad_branch = (alive_rows * grad_after_self).astype(jnp.bfloat16)
    order.mark(grad_branch)
    down_sum.advance()
    grad_attended = times_transposed(order.hold(grad_branch), output_weight).astype(jnp.bfloat16)
    grad_mixed = self_backward(mixed_rows, grad_attended, logs_self, heads, heads_block, scale)
    order.mark(grad_mixed)
    grad_normed_self = times_transposed(order.hold(grad_mixed), mixed_weight)
    grad_rows, grad_self_gain = norm_backward(grad_normed_self, unit_self, inverse_self, self_gain)
    grad_after_cross = grad_after_self + grad_rows
    grad_cross_blocks = gather_blocks((alive_rows * grad_after_cross).astype(jnp.bfloat16))
    order.mark(grad_cross_blocks[0])

    up_sum.advance()
    down_sum.advance()
    late_mixed = order.hold(grad_mixed)
    self_terms = []
    for step in range(tp_count):
        terms = [
            transposed_times(
                normed_self, late_mixed[:, (3 * step + kind) * width : (3 * step + kind + 1) * width]
            ).astype(jnp.bfloat16)
            for kind in range(3)
        ]
        output_term = transposed_times(
            attended_self[:, step * width : (step + 1) * width], grad_branch
        ).astype(jnp.bfloat16)
        self_terms.append(terms + [stack_output(output_term)])
    self_sums = [
        SetSum(
            order,
            order.hold(jnp.stack([jnp.stack(terms[first : first + 2]) for terms in self_terms])),
            halve,
            layout=natural,
            peers_after=peers_after,
            double=False,
        )
        for first, halve, peers_after in ((0, bits, 1), (2, bits, len(bits)))
    ]

    grad_queries, sums = [], ()
    for step in range(tp_count):
        block = order.hold(grad_cross_blocks[step])
        grad_attended = times_transposed(block, cross_output).astype(jnp.bfloat16)
        grad_query, *sums = cross_backward(
            log_counts,
            queries_cross[step],
            grad_attended,
            logs_cross[step],
            key_table,
            key_table_t,
            value_table,
            scale,
            step * local_groups,
            tuple(sums),
            step == tp_count - 1,
        )
        grad_queries.append(grad_query)
        order.mark(grad_query)
        if step == 0:
            up_sum.advance()
            down_sum.advance()
            self_sums[1].advance()
            self_sums[0].advance()
    grad_key_table, grad_value_table = sums
    while up_sum.stages or down_sum.stages:
        up_sum.advance()
        down_sum.advance()
    feed_result = lax.all_gather(
        jnp.concatenate([up_sum.block, down_sum.block], axis=0), "sets", axis=1, tiled=True
    )
    held_keys, held_values = order.hold((grad_key_table, grad_value_table))
    grad_key = transposed_times(embedded, held_keys).astype(jnp.bfloat16)
    grad_value = transposed_times(embedded, held_values).astype(jnp.bfloat16)
    first_sum = SetSum(order, jnp.stack([grad_key, grad_value]), bits)
    self_sums[1].advance()
    output_terms, query_terms = [], []
    for step in range(tp_count):
        output_terms.append(
            transposed_times(attended_cross[step], order.hold(grad_cross_blocks[step]))
        )
        query_terms.append(transposed_times(rows_cross[step], order.hold(grad_queries[step])))
    grad_query = functools.reduce(jnp.add, query_terms).astype(jnp.bfloat16)
    grad_output = functools.reduce(jnp.add, output_terms).astype(jnp.bfloat16)
    second_sum = SetSum(order, jnp.stack([grad_query, stack_output(grad_output)]), cross_first)
    self_sums[0].advance()
    first_sum.advance()
    second_sum.advance()

    def query_term(step):
        return times_transposed(order.hold(grad_queries[step]), cross_query)

    def input_term(step):
        keys, values = order.hold(
            (table_part(grad_key_table, step), table_part(grad_value_table, step))
        )
        return times_transposed(keys, cross_key) + times_transposed(values, cross_value)

    query_sums, input_sums, final_terms = [], [], []
    for step in range(1, tp_count):
        term = query_term(step).astype(jnp.bfloat16)
        query_sums.append(to_peer(term, step))
        order.mark(term)
    grad_normed_cross = query_term(0)
    order.mark(grad_normed_cross)
    def advance_all(*totals):
        for total in totals:
            total.advance()

    final_all = project(order.hold(activated), feed_down)
    for step in range(1, tp_count):
        term = block_rows(final_all, step).astype(jnp.bfloat16)
        final_terms.append(to_peer(term, step))
        order.mark(term)
    advance_all(self_sums[1], self_sums[0], first_sum, second_sum)
    for step in range(1, tp_count):
        term = input_term(step).astype(jnp.bfloat16)
        input_sums.append(to_peer(term, step))
        order.mark(term)
    advance_all(self_sums[1], self_sums[0], first_sum, second_sum)
    for term in order.hold(tuple(query_sums)):
        grad_normed_cross = grad_normed_cross + term.astype(jnp.float32)
    grad_rows, grad_cross_gain = norm_backward(
        grad_normed_cross, unit_cross, inverse_cross, cross_gain
    )
    latent_grad = grad_after_cross + grad_rows
    order.mark(latent_grad)
    while any(total.stages for total in self_sums):
        advance_all(self_sums[1], self_sums[0])
    self_result = lax.all_gather(
        jnp.concatenate([total.block for total in self_sums], axis=0), "sets", axis=1, tiled=True
    )
    final_rows = block_rows(final_all, 0)
    for term in order.hold(tuple(final_terms)):
        final_rows = final_rows + term.astype(jnp.float32)
    final_rows = after_self + alive_rows * final_rows
    group_rms = jnp.sqrt(jnp.mean((final_rows * final_rows).reshape(local_groups, -1), axis=1))
    penalty_term = jnp.sum(group_rms * group_alive)
    order.mark(final_rows)
    small = jnp.stack(
        [
            grad_feed_gain,
            grad_self_gain,
            jnp.full_like(grad_feed_gain, penalty_term),
            grad_cross_gain,
        ],
        axis=0,
    )
    spots = [("sets", 1 << bit) for bit in bits]
    step = 1
    while step < tp_count:
        spots.append(("tp", step))
        step *= 2

    def small_step():
        nonlocal small
        if spots:
            axis, step = spots.pop(0)
            received = lax.ppermute(
                small, axis, [(place, place ^ step) for place in range(lax.axis_size(axis))]
            )
            small = small + order.hold(received)
            order.mark(small)

    running = [first_sum, second_sum]
    advance_all(*running)
    small_step()
    up_blocks = hidden_width // feed_width
    feed_result = order.hold(feed_result)
    grad_feed_up = jnp.concatenate(
        [feed_result[place] for place in range(up_blocks)], axis=1
    ).astype(jnp.float32)
    if hidden_width >= model:
        grad_feed_down = feed_result[up_blocks:].reshape(hidden_width, model).astype(jnp.float32)
    else:
        grad_feed_down = unstack_output(feed_result[up_blocks]).astype(jnp.float32)
    order.mark(grad_feed_up, grad_feed_down)
    advance_all(*running)
    small_step()
    input_grad = input_term(0)
    for term in order.hold(tuple(input_sums)):
        input_grad = input_grad + term.astype(jnp.float32)
    order.mark(input_grad)
    while any(total.stages for total in running) or spots:
        advance_all(*running)
        small_step()
    grad_self_query, grad_self_key, grad_self_value = [
        self_result[kind].astype(jnp.float32) for kind in range(3)
    ]
    grad_self_output = unstack_output(self_result[3]).astype(jnp.float32)
    grad_cross_key, grad_cross_value = first_sum.result(0), first_sum.result(1)
    grad_cross_query = second_sum.result(0)
    grad_cross_output = unstack_output(second_sum.result(1))
    grad_feed_gain, grad_self_gain, _, grad_cross_gain = [small[place] for place in range(4)]
    penalty = small[2, 0] / (group_count * lax.axis_size("sets"))
    return (
        final_rows.astype(jnp.bfloat16),
        latent_grad,
        input_grad,
        grad_cross_gain,
        grad_cross_query,
        grad_cross_key,
        grad_cross_value,
        grad_cross_output,
        grad_self_gain,
        grad_self_query,
        grad_self_key,
        grad_self_value,
        grad_self_output,
        grad_feed_gain,
        grad_feed_up,
        grad_feed_down,
        penalty,
    )


def solution(mesh):
    return jax.shard_map(
        local,
        mesh=mesh,
        in_specs=(
            P(("sets", "tp"), None),
            P(("sets", "tp"), None),
            P("sets", None),
            P("sets"),
            P("sets"),
            P(("sets", "tp"), None),
            P(),
            P(None, "tp"),
            P(None, "tp"),
            P(None, "tp"),
            P("tp", None),
            P(),
            P(None, "tp"),
            P(None, "tp"),
            P(None, "tp"),
            P("tp", None),
            P(),
            P(None, "tp"),
            P("tp", None),
        ),
        out_specs=(
            P(("sets", "tp"), None),
            P(("sets", "tp"), None),
            P(("sets", "tp"), None),
            P(),
            P(None, "tp"),
            P(None, "tp"),
            P(None, "tp"),
            P("tp", None),
            P(),
            P(None, "tp"),
            P(None, "tp"),
            P(None, "tp"),
            P("tp", None),
            P(),
            P(None, "tp"),
            P("tp", None),
            P(),
        ),
        check_vma=False,
    )
```

```python
import functools
import math

import jax
import jax.numpy as jnp
from jax import lax
from jax.experimental import pallas as pl
from jax.experimental.pallas import tpu as pltpu
from jax.sharding import PartitionSpec as P

HEAD_DIM = 128
GROUP = 128

epsilon = 1e-05
masked_score = -1e30
gelu_factor = 0.7978845608028654
gelu_cubic = 0.044715
log2_e = 1.4426950408889634
vmem_bytes = 60 * 1024 * 1024
small_cost = pl.CostEstimate(flops=1000000, transcendentals=1000, bytes_accessed=100000)


def project(left_rows, right_rows):
    return jnp.dot(left_rows, right_rows, preferred_element_type=jnp.float32)


def times_transposed(left_rows, right_rows):
    return lax.dot_general(
        left_rows, right_rows, (((1,), (1,)), ((), ())), preferred_element_type=jnp.float32
    )


def transposed_times(left_rows, right_rows):
    return lax.dot_general(
        left_rows, right_rows, (((0,), (0,)), ((), ())), preferred_element_type=jnp.float32
    )


def norm_forward(values, gain):
    average = jnp.mean(values, axis=1, keepdims=True)
    centred = values - average
    variance = jnp.mean(centred * centred, axis=1, keepdims=True)
    inverse = lax.rsqrt(variance + epsilon)
    unit_rows = centred * inverse
    return (unit_rows, inverse, (unit_rows * gain).astype(jnp.bfloat16))


def norm_backward(grad_normed, unit_rows, inverse, gain):
    scaled = grad_normed * gain
    first_mean = jnp.mean(scaled, axis=1, keepdims=True)
    second_mean = jnp.mean(scaled * unit_rows, axis=1, keepdims=True)
    grad_rows = inverse * (scaled - first_mean - unit_rows * second_mean)
    return (grad_rows, jnp.sum(grad_normed * unit_rows, axis=0))


def from_peer(block, step):
    count = lax.axis_size("tp")
    return lax.ppermute(block, "tp", [(source, (source - step) % count) for source in range(count)])


def to_peer(block, step):
    count = lax.axis_size("tp")
    return lax.ppermute(block, "tp", [(source, (source + step) % count) for source in range(count)])


def gather_blocks(block):
    return [block] + [from_peer(block, step) for step in range(1, lax.axis_size("tp"))]


def sum_blocks(make_partial):
    received = [
        to_peer(make_partial(step).astype(jnp.bfloat16), step)
        for step in range(1, lax.axis_size("tp"))
    ]
    total = make_partial(0)
    for term in received:
        total = total + term.astype(jnp.float32)
    return total


def swap_sets(block, bit):
    count = lax.axis_size("sets")
    return lax.ppermute(block, "sets", [(source, source ^ (1 << bit)) for source in range(count)])


def set_bit(bit):
    return (lax.axis_index("sets") >> bit) & 1


def halves(block, bit, before=0):
    rows, columns = block.shape[-2:]
    lead = block.shape[:-2]
    view = block.reshape(lead + (2**before, 2, rows // 2 ** (before + 1), columns))
    axis = view.ndim - 3
    mine = set_bit(bit)
    kept, sent = [
        lax.dynamic_slice_in_dim(view, place, 1, axis).reshape(lead + (rows // 2, columns))
        for place in (mine, 1 - mine)
    ]
    return (kept, sent)


def add_pair(kept, received):
    return (kept.astype(jnp.float32) + received.astype(jnp.float32)).astype(jnp.bfloat16)


class Order:
    def __init__(self):
        self.last = ()

    def hold(self, value):
        if not self.last:
            return value
        return lax.optimization_barrier((value, *self.last))[0]

    def mark(self, *values):
        self.last = values


def join(block, received, bit):
    first = set_bit(bit) == 0
    return jnp.concatenate(
        [jnp.where(first, block, received), jnp.where(first, received, block)],
        axis=block.ndim - 2,
    )


def all_bits():
    return list(range(int(math.log2(lax.axis_size("sets")))))


class SetSum:
    def __init__(self, order, block, halve, layout=None, peers_after=None, double=True):
        self.order = order
        self.block = block.astype(jnp.bfloat16)
        self.layout = list(halve if layout is None else layout)
        self.stages = [("halve", bit) for bit in halve]
        if peers_after is not None:
            self.stages.insert(peers_after, ("peers", None))
        if double:
            self.stages += [("double", bit) for bit in reversed(halve)]
        self.last = None
        self.send()

    def send(self):
        kind, bit = self.stages[0]
        if kind == "halve":
            before = self.layout.index(bit)
            self.layout.remove(bit)
            self.kept, sent = halves(self.block, bit, before)
            self.received = [swap_sets(sent, bit)]
        elif kind == "peers":
            self.kept = self.block[0]
            sent = [self.block[step] for step in range(1, self.block.shape[0])]
            self.received = [to_peer(part, step + 1) for step, part in enumerate(sent)]
            self.order.mark(*sent)
            return
        else:
            self.kept = sent = self.block
            self.received = [swap_sets(sent, bit)]
        self.order.mark(sent)

    def advance(self):
        if not self.stages:
            return
        kind, bit = self.stages.pop(0)
        received = self.order.hold(tuple(self.received))
        if kind == "double" and not self.stages:
            self.last = (self.kept, received[0], bit)
            self.order.mark(received[0])
            return
        if kind == "double":
            self.block = join(self.kept, received[0], bit)
        else:
            total = self.kept.astype(jnp.float32)
            for term in received:
                total = total + term.astype(jnp.float32)
            self.block = total.astype(jnp.bfloat16)
        if self.stages:
            self.send()
        else:
            self.order.mark(self.block)

    def result(self, place=None):
        kept, received, bit = self.last
        if place is not None:
            kept, received = kept[place], received[place]
        return join(kept, received, bit).astype(jnp.float32)


def stack_output(weight):
    width = weight.shape[0]
    return jnp.concatenate(
        [weight[:, start : start + width] for start in range(0, weight.shape[1], width)], axis=0
    )


def unstack_output(stacked):
    width = stacked.shape[1]
    return jnp.concatenate(
        [stacked[start : start + width] for start in range(0, stacked.shape[0], width)], axis=1
    )


def multiplicity_kernel(chosen_ref, out_ref):
    row_count = out_ref.shape[0]
    group_count, key_count = chosen_ref.shape
    row_ids = lax.broadcasted_iota(jnp.int32, (row_count, key_count), 0) + (
        pl.program_id(0) * row_count
    )
    lanes = lax.broadcasted_iota(jnp.int32, (key_count, 128), 1)

    def one_group(group, total):
        picked = chosen_ref[pl.ds(group, 1), :]
        hits = jnp.where(row_ids == picked, 1.0, 0.0).astype(jnp.bfloat16)
        place = jnp.where(lanes == group, 1.0, 0.0).astype(jnp.bfloat16)
        return total + project(hits, place)

    total = lax.fori_loop(0, group_count, one_group, jnp.zeros((row_count, 128), jnp.float32))
    out_ref[...] = jnp.where(total > 0.0, jnp.log2(jnp.maximum(total, 1.0)), masked_score)


def log_multiplicity(chosen, counts, table_rows):
    group_count, key_count = chosen.shape
    valid = jnp.arange(key_count, dtype=jnp.int32)[None, :] < counts[:, None]
    chosen = jnp.where(valid, chosen, -1)
    block = math.gcd(table_rows, 512)
    return pl.pallas_call(
        multiplicity_kernel,
        grid=(table_rows // block,),
        in_specs=[pl.BlockSpec((group_count, key_count), lambda i: (0, 0))],
        out_specs=pl.BlockSpec((block, 128), lambda i: (i, 0)),
        out_shape=jax.ShapeDtypeStruct((table_rows, 128), jnp.float32),
        name="multiplicity",
    )(chosen)


def fill_bias(counts_ref, bias_ref, span, first_group):
    row_count = bias_ref.shape[0]
    lanes = lax.broadcasted_iota(jnp.int32, (row_count, 128), 1)
    counts = counts_ref[...]
    for part in range(span):
        group = first_group + pl.program_id(0) * span + part
        column = jnp.sum(jnp.where(lanes == group, counts, 0.0), axis=1, keepdims=True)
        bias_ref[:, part * GROUP : (part + 1) * GROUP] = jnp.broadcast_to(
            column, (row_count, GROUP)
        )


def cross_forward_kernel(
    counts_ref,
    rows_ref,
    key_ref,
    value_t_ref,
    query_weight_ref,
    output_weight_ref,
    query_ref,
    out_ref,
    log_ref,
    branch_ref,
    bias_ref,
    *,
    heads,
    span,
    scale,
    first_group,
):
    fill_bias(counts_ref, bias_ref, span, first_group)
    query_ref[...] = project(rows_ref[...], query_weight_ref[...]).astype(jnp.bfloat16)
    for head in range(heads):
        cols = slice(head * HEAD_DIM, (head + 1) * HEAD_DIM)
        scores = times_transposed(key_ref[:, cols], query_ref[:, cols])
        scores = scores * (scale * log2_e) + bias_ref[...]
        top = jnp.max(scores, axis=0, keepdims=True)
        raised = jnp.exp2(scores - top)
        total = jnp.sum(raised, axis=0, keepdims=True)
        mixed = project(value_t_ref[cols, :], raised.astype(jnp.bfloat16)) / total
        out_ref[:, cols] = mixed.T.astype(jnp.bfloat16)
        log_ref[0, head : head + 1, :] = top + jnp.log2(total)
    branch_ref[...] = project(out_ref[...], output_weight_ref[...]).astype(branch_ref.dtype)


def cross_forward(
    log_counts,
    normed,
    key_table,
    value_table_t,
    query_weight,
    output_weight,
    scale,
    first_group,
    branch_type,
):
    row_count, model = normed.shape
    table_rows, width = key_table.shape
    heads = width // HEAD_DIM
    groups = row_count // GROUP
    span = 2 if groups % 2 == 0 else 1
    rows = span * GROUP
    block = pl.BlockSpec((rows, width), lambda i: (i, 0))
    wide_block = pl.BlockSpec((rows, model), lambda i: (i, 0))
    return pl.pallas_call(
        functools.partial(
            cross_forward_kernel, heads=heads, span=span, scale=scale, first_group=first_group
        ),
        grid=(groups // span,),
        in_specs=[
            pl.BlockSpec((table_rows, 128), lambda i: (0, 0)),
            wide_block,
            pl.BlockSpec((table_rows, width), lambda i: (0, 0)),
            pl.BlockSpec((width, table_rows), lambda i: (0, 0)),
            pl.BlockSpec((model, width), lambda i: (0, 0)),
            pl.BlockSpec((width, model), lambda i: (0, 0)),
        ],
        out_specs=[block, block, pl.BlockSpec((1, heads, rows), lambda i: (i, 0, 0)), wide_block],
        out_shape=[
            jax.ShapeDtypeStruct((row_count, width), jnp.bfloat16),
            jax.ShapeDtypeStruct((row_count, width), jnp.bfloat16),
            jax.ShapeDtypeStruct((groups // span, heads, rows), jnp.float32),
            jax.ShapeDtypeStruct((row_count, model), branch_type),
        ],
        scratch_shapes=[pltpu.VMEM((table_rows, rows), jnp.float32)],
        compiler_params=pltpu.CompilerParams(vmem_limit_bytes=vmem_bytes),
        cost_estimate=small_cost,
        name="cross_forward",
    )(log_counts, normed, key_table, value_table_t, query_weight, output_weight)


def cross_backward_kernel(*refs, heads, span, scale, first_group, start, finish):
    counts_ref, query_ref, grad_ref, log_ref, key_ref, key_t_ref, value_ref = refs[:7]
    refs = refs[7:]
    if not start:
        key_start_ref, value_start_ref = refs[:2]
        refs = refs[2:]
    grad_query_ref, grad_key_ref, grad_value_ref, bias_ref = refs[:4]
    key_sum_ref, value_sum_ref = refs[4:] if finish else (grad_key_ref, grad_value_ref)
    step = pl.program_id(0)

    @pl.when(step == 0)
    def _():
        if start:
            key_sum_ref[...] = jnp.zeros_like(key_sum_ref)
            value_sum_ref[...] = jnp.zeros_like(value_sum_ref)
        else:
            key_sum_ref[...] = key_start_ref[...]
            value_sum_ref[...] = value_start_ref[...]

    fill_bias(counts_ref, bias_ref, span, first_group)
    for head in range(heads):
        cols = slice(head * HEAD_DIM, (head + 1) * HEAD_DIM)
        query = query_ref[:, cols]
        grad = grad_ref[:, cols]
        scores = times_transposed(key_ref[:, cols], query)
        weights = jnp.exp2(
            scores * (scale * log2_e) + bias_ref[...] - log_ref[0, head : head + 1, :]
        )
        grad_weights = times_transposed(value_ref[:, cols], grad)
        inner = jnp.sum(weights * grad_weights, axis=0, keepdims=True)
        grad_scores = (weights * (grad_weights - inner)).astype(jnp.bfloat16)
        value_sum_ref[:, cols] += project(weights.astype(jnp.bfloat16), grad)
        key_sum_ref[:, cols] += project(grad_scores, query)
        grad_query = project(key_t_ref[cols, :], grad_scores) * scale
        grad_query_ref[:, cols] = grad_query.T.astype(jnp.bfloat16)

    if finish:

        @pl.when(step == pl.num_programs(0) - 1)
        def _():
            grad_key_ref[...] = (key_sum_ref[...] * scale).astype(jnp.bfloat16)
            grad_value_ref[...] = value_sum_ref[...].astype(jnp.bfloat16)


def cross_backward(
    log_counts,
    queries,
    grad_attended,
    logs,
    key_table,
    key_table_t,
    value_table,
    scale,
    first_group,
    earlier,
    finish,
):
    row_count, width = queries.shape
    table_rows = key_table.shape[0]
    heads = width // HEAD_DIM
    groups = row_count // GROUP
    span = 2 if groups % 2 == 0 else 1
    rows = span * GROUP
    whole = pl.BlockSpec((table_rows, width), lambda i: (0, 0))
    block = pl.BlockSpec((rows, width), lambda i: (i, 0))
    table_type = jnp.bfloat16 if finish else jnp.float32
    sums = pltpu.VMEM((table_rows, width), jnp.float32)
    return pl.pallas_call(
        functools.partial(
            cross_backward_kernel,
            heads=heads,
            span=span,
            scale=scale,
            first_group=first_group,
            start=not earlier,
            finish=finish,
        ),
        grid=(groups // span,),
        in_specs=[
            pl.BlockSpec((table_rows, 128), lambda i: (0, 0)),
            block,
            block,
            pl.BlockSpec((1, heads, rows), lambda i: (i, 0, 0)),
            whole,
            pl.BlockSpec((width, table_rows), lambda i: (0, 0)),
            whole,
        ]
        + [whole] * len(earlier),
        out_specs=[block, whole, whole],
        out_shape=[
            jax.ShapeDtypeStruct((row_count, width), jnp.bfloat16),
            jax.ShapeDtypeStruct((table_rows, width), table_type),
            jax.ShapeDtypeStruct((table_rows, width), table_type),
        ],
        scratch_shapes=[pltpu.VMEM((table_rows, rows), jnp.float32)]
        + ([sums, sums] if finish else []),
        compiler_params=pltpu.CompilerParams(vmem_limit_bytes=vmem_bytes),
        cost_estimate=small_cost,
        name="cross_backward",
    )(log_counts, queries, grad_attended, logs, key_table, key_table_t, value_table, *earlier)


def head_columns(head, heads_block):
    base = (head // heads_block) * 3 * heads_block + head % heads_block
    return [
        slice((base + kind * heads_block) * HEAD_DIM, (base + kind * heads_block + 1) * HEAD_DIM)
        for kind in range(3)
    ]


def norm_block(values, gain, average_ref, inverse_ref):
    average = jnp.mean(values, axis=1, keepdims=True)
    centred = values - average
    variance = jnp.mean(centred * centred, axis=1, keepdims=True)
    inverse = lax.rsqrt(variance + epsilon)
    average_ref[...] = average
    inverse_ref[...] = inverse
    return (centred * inverse * gain).astype(jnp.bfloat16)


def self_forward_kernel(
    state_ref,
    alive_ref,
    self_gain_ref,
    feed_gain_ref,
    mixed_weight_ref,
    output_weight_ref,
    normed_ref,
    rows_ref,
    out_ref,
    log_ref,
    after_ref,
    feed_ref,
    self_average_ref,
    self_inverse_ref,
    feed_average_ref,
    feed_inverse_ref,
    *,
    heads,
    heads_block,
    scale,
):
    normed_ref[...] = norm_block(
        state_ref[...], self_gain_ref[...], self_average_ref, self_inverse_ref
    )
    rows_ref[...] = project(normed_ref[...], mixed_weight_ref[...]).astype(jnp.bfloat16)
    columns = [head_columns(head, heads_block) for head in range(heads)]
    for group in range(state_ref.shape[0] // GROUP):
        rows = slice(group * GROUP, (group + 1) * GROUP)
        scores = [
            times_transposed(rows_ref[rows, key_cols], rows_ref[rows, query_cols])
            for query_cols, key_cols, _ in columns
        ]
        weights = []
        for head in range(heads):
            scaled = scores[head] * (scale * log2_e)
            top = jnp.max(scaled, axis=0, keepdims=True)
            raised = jnp.exp2(scaled - top)
            total = jnp.sum(raised, axis=0, keepdims=True)
            weights.append((raised * (1.0 / total)).astype(jnp.bfloat16))
            log_ref[group, head : head + 1, :] = top + jnp.log2(total)
        for head in range(heads):
            mixed = transposed_times(weights[head], rows_ref[rows, columns[head][2]])
            out_ref[rows, head * HEAD_DIM : (head + 1) * HEAD_DIM] = mixed.astype(jnp.bfloat16)
    branch = project(out_ref[...], output_weight_ref[...])
    after_ref[...] = state_ref[...] + alive_ref[...] * branch
    feed_ref[...] = norm_block(
        after_ref[...], feed_gain_ref[...], feed_average_ref, feed_inverse_ref
    )


def self_forward(
    state_rows, alive_rows, self_gain, feed_gain, mixed_weight, output_weight, heads, heads_block, scale
):
    row_count, model = state_rows.shape
    groups = row_count // GROUP
    span = 2 if groups % 2 == 0 else 1
    rows = span * GROUP
    mixed_width = mixed_weight.shape[1]

    def block(width):
        return pl.BlockSpec((rows, width), lambda i: (i, 0))

    def whole(array):
        return pl.BlockSpec(array.shape, lambda i: (0, 0))

    def result(width, kind):
        return jax.ShapeDtypeStruct((row_count, width), kind)

    weights = (self_gain[None], feed_gain[None], mixed_weight, output_weight)
    return pl.pallas_call(
        functools.partial(
            self_forward_kernel, heads=heads, heads_block=heads_block, scale=scale
        ),
        grid=(groups // span,),
        in_specs=[block(model), block(1)] + [whole(array) for array in weights],
        out_specs=[
            block(model),
            block(mixed_width),
            block(heads * HEAD_DIM),
            pl.BlockSpec((span, heads, GROUP), lambda i: (i, 0, 0)),
            block(model),
            block(model),
        ]
        + [block(1)] * 4,
        out_shape=[
            result(model, jnp.bfloat16),
            result(mixed_width, jnp.bfloat16),
            result(heads * HEAD_DIM, jnp.bfloat16),
            jax.ShapeDtypeStruct((groups, heads, GROUP), jnp.float32),
            result(model, jnp.float32),
            result(model, jnp.bfloat16),
        ]
        + [result(1, jnp.float32)] * 4,
        compiler_params=pltpu.CompilerParams(vmem_limit_bytes=vmem_bytes),
        cost_estimate=small_cost,
        name="self_forward",
    )(state_rows, alive_rows, *weights)


def self_backward_kernel(rows_ref, grad_ref, log_ref, out_ref, *, heads, heads_block, scale):
    columns = [head_columns(head, heads_block) for head in range(heads)]
    grads = [slice(head * HEAD_DIM, (head + 1) * HEAD_DIM) for head in range(heads)]
    scores = [
        times_transposed(rows_ref[:, key_cols], rows_ref[:, query_cols])
        for query_cols, key_cols, _ in columns
    ]
    grad_weights = [
        times_transposed(rows_ref[:, columns[head][2]], grad_ref[:, grads[head]])
        for head in range(heads)
    ]
    weights, grad_scores = [], []
    for head in range(heads):
        soft = jnp.exp2(scores[head] * (scale * log2_e) - log_ref[0, head : head + 1, :])
        inner = jnp.sum(soft * grad_weights[head], axis=0, keepdims=True)
        grad_scores.append((soft * (grad_weights[head] - inner)).astype(jnp.bfloat16))
        weights.append(soft.astype(jnp.bfloat16))
    for head in range(heads):
        query_cols, key_cols, value_cols = columns[head]
        out_ref[:, value_cols] = project(weights[head], grad_ref[:, grads[head]]).astype(
            jnp.bfloat16
        )
        out_ref[:, key_cols] = (project(grad_scores[head], rows_ref[:, query_cols]) * scale).astype(
            jnp.bfloat16
        )
        out_ref[:, query_cols] = (
            transposed_times(grad_scores[head], rows_ref[:, key_cols]) * scale
        ).astype(jnp.bfloat16)


def self_backward(mixed_rows, grad_attended, logs, heads, heads_block, scale):
    row_count, width = mixed_rows.shape
    groups = row_count // GROUP
    return pl.pallas_call(
        functools.partial(
            self_backward_kernel, heads=heads, heads_block=heads_block, scale=scale
        ),
        grid=(groups,),
        in_specs=[
            pl.BlockSpec((GROUP, width), lambda i: (i, 0)),
            pl.BlockSpec((GROUP, heads * HEAD_DIM), lambda i: (i, 0)),
            pl.BlockSpec((1, heads, GROUP), lambda i: (i, 0, 0)),
        ],
        out_specs=pl.BlockSpec((GROUP, width), lambda i: (i, 0)),
        out_shape=jax.ShapeDtypeStruct((row_count, width), jnp.bfloat16),
        cost_estimate=small_cost,
        name="self_backward",
    )(mixed_rows, grad_attended, logs)


def feed_kernel(rows_ref, grad_ref, up_ref, down_ref, *rest):
    active_ref, grad_hidden_ref, grad_rows_ref, sum_ref = rest[-4:]
    step = pl.program_id(0)

    @pl.when(step == 0)
    def _():
        sum_ref[...] = jnp.zeros_like(sum_ref)

    hidden = project(rows_ref[...], up_ref[...])
    grad_active = times_transposed(grad_ref[...], down_ref[...])
    square = hidden * hidden
    bend = jnp.tanh(gelu_factor * hidden * (1.0 + gelu_cubic * square))
    half_sum = 0.5 * (1.0 + bend)
    slope = half_sum + (0.5 * gelu_factor) * hidden * (1.0 - bend * bend) * (
        1.0 + (3.0 * gelu_cubic) * square
    )
    grad_hidden = (slope * grad_active).astype(jnp.bfloat16)
    active_ref[...] = (hidden * half_sum).astype(jnp.bfloat16)
    grad_hidden_ref[...] = grad_hidden
    sum_ref[...] += times_transposed(grad_hidden, up_ref[...])

    @pl.when(step == pl.num_programs(0) - 1)
    def _():
        grad_rows_ref[...] = sum_ref[...].astype(grad_rows_ref.dtype)


def feed_block(first_row, total_rows, rows, grads, up, down, earlier, sum_type):
    row_count, width = rows.shape
    hidden_width = up.shape[1]
    tile = math.gcd(hidden_width, 512)
    place = first_row // row_count
    result = jax.ShapeDtypeStruct((total_rows, hidden_width), jnp.bfloat16)
    block = pl.BlockSpec((row_count, tile), lambda i: (place, i))
    whole = pl.BlockSpec((row_count, width), lambda i: (0, 0))
    return pl.pallas_call(
        feed_kernel,
        grid=(hidden_width // tile,),
        in_specs=[
            whole,
            whole,
            pl.BlockSpec((width, tile), lambda i: (0, i)),
            pl.BlockSpec((tile, width), lambda i: (i, 0)),
        ]
        + [pl.BlockSpec(memory_space=pl.ANY)] * len(earlier),
        out_specs=[block, block, whole],
        out_shape=[result, result, jax.ShapeDtypeStruct((row_count, width), sum_type)],
        scratch_shapes=[pltpu.VMEM((row_count, width), jnp.float32)],
        input_output_aliases={4: 0, 5: 1} if earlier else {},
        compiler_params=pltpu.CompilerParams(vmem_limit_bytes=vmem_bytes),
        cost_estimate=small_cost,
        name="feed_hidden",
    )(rows, grads, up, down, *earlier)


def local(
    latents,
    inputs,
    neighbours,
    key_counts,
    filled,
    cotangent,
    cross_gain,
    cross_query,
    cross_key,
    cross_value,
    cross_output,
    self_gain,
    self_query,
    self_key,
    self_value,
    self_output,
    feed_gain,
    feed_up,
    feed_down,
):
    tp_count = lax.axis_size("tp")
    tp_index = lax.axis_index("tp")
    bits = all_bits()
    rows_dev = latents.shape[0]
    table_dev = inputs.shape[0]
    table_rows = table_dev * tp_count
    group_count = neighbours.shape[0]
    local_groups = rows_dev // GROUP
    scale = 1.0 / math.sqrt(HEAD_DIM)
    first_group = tp_index * local_groups
    group_alive = (first_group + jnp.arange(local_groups, dtype=jnp.int32) < filled[0]).astype(
        jnp.float32
    )
    alive_rows = jnp.repeat(group_alive, GROUP)[:, None]

    chosen = jnp.roll(neighbours, -first_group, axis=0)
    counts = jnp.roll(key_counts, -first_group, axis=0)
    chosen = (chosen - tp_index * table_dev) % table_rows
    log_counts = log_multiplicity(chosen, counts, table_rows)

    def block_rows(array, step):
        return array[step * rows_dev : (step + 1) * rows_dev]

    def table_part(array, step):
        return array[step * table_dev : (step + 1) * table_dev]

    heads_block = self_query.shape[1] // HEAD_DIM
    heads = heads_block * tp_count
    width = heads_block * HEAD_DIM
    model = self_query.shape[0]
    hidden_width = feed_up.shape[1]
    feed_width = min(hidden_width, model)
    cross_first = bits[:1] + bits[2:] + bits[1:2]
    natural = list(reversed(bits))
    order = Order()

    piece_rows = rows_dev // 2 if local_groups % 2 == 0 else rows_dev
    piece_starts = list(range(0, rows_dev, piece_rows))

    def pieces(block):
        return [block[start : start + piece_rows] for start in piece_starts]

    peer_inputs = gather_blocks(inputs)
    own_slice = jnp.stack([self_query, self_key, self_value, stack_output(self_output)], axis=0)
    share = model // lax.axis_size("sets")
    own_slice = lax.dynamic_slice_in_dim(own_slice, lax.axis_index("sets") * share, share, 1)
    peer_slices = [from_peer(own_slice, step) for step in range(1, tp_count)]

    state_rows = latents.astype(jnp.float32)
    grad_final = cotangent.astype(jnp.float32)
    grad_own = (alive_rows * grad_final).astype(jnp.bfloat16)
    unit_cross, inverse_cross, normed_cross = norm_forward(state_rows, cross_gain)
    order.mark(normed_cross)
    log_counts = log_multiplicity(order.hold(chosen), counts, table_rows)
    order.mark(log_counts)
    peer_inputs = order.hold(tuple(peer_inputs))
    order.mark(*peer_inputs)
    rows_cross = gather_blocks(order.hold(normed_cross))
    embedded = jnp.concatenate(peer_inputs, axis=0)
    order.mark(embedded)
    peer_stacks = [
        lax.all_gather(part, "sets", axis=1, tiled=True) for part in order.hold(tuple(peer_slices))
    ]
    key_table = project(order.hold(embedded), cross_key).astype(jnp.bfloat16)
    value_table_t = lax.dot_general(
        cross_value, embedded, (((0,), (1,)), ((), ())), preferred_element_type=jnp.float32
    ).astype(jnp.bfloat16)
    order.mark(key_table, value_table_t)
    grad_pieces = [[] for _ in range(tp_count)]
    queries_cross, attended_cross, logs_cross, cross_terms = [], [], [], []
    for step in range(tp_count):
        rows = order.hold(rows_cross[step])
        order.mark(rows)
        if step == tp_count - 1:
            for peer in range(1, tp_count):
                grad_pieces[peer].append(from_peer(order.hold(pieces(grad_own)[0]), peer))
        queries, attended, logs, term = cross_forward(
            log_counts,
            rows,
            key_table,
            value_table_t,
            cross_query,
            cross_output,
            scale,
            step * local_groups,
            jnp.bfloat16 if step else jnp.float32,
        )
        queries_cross.append(queries)
        attended_cross.append(attended)
        logs_cross.append(logs)
        if step == 0:
            branch = term
            order.mark(attended)
        else:
            cross_terms.append(to_peer(term, step))
            order.mark(term)
        if step == tp_count - 1:
            for peer in range(1, tp_count):
                grad_pieces[peer][0] = order.hold(grad_pieces[peer][0])
            order.mark(term, *[parts[0] for parts in grad_pieces[1:]])
    key_table_t = lax.dot_general(
        cross_key, order.hold(embedded), (((0,), (1,)), ((), ())), preferred_element_type=jnp.float32
    ).astype(jnp.bfloat16)
    value_table = project(order.hold(embedded), cross_value).astype(jnp.bfloat16)
    order.mark(key_table_t, value_table)
    peer_stacks = order.hold(tuple(peer_stacks))
    mixed_weight = jnp.concatenate(
        [self_query, self_key, self_value]
        + [stack[kind] for stack in peer_stacks for kind in range(3)],
        axis=1,
    )
    output_weight = jnp.concatenate(
        [self_output] + [unstack_output(stack[3]) for stack in peer_stacks], axis=0
    )
    mixed_weight, output_weight = lax.optimization_barrier((mixed_weight, output_weight))
    order.mark(mixed_weight, output_weight)
    for term in order.hold(tuple(cross_terms)):
        branch = branch + term.astype(jnp.float32)
    after_cross = state_rows + alive_rows * branch
    order.mark(after_cross)

    for piece in pieces(grad_own)[1:]:
        for step in range(1, tp_count):
            grad_pieces[step].append(from_peer(order.hold(piece), step))
    (
        normed_self,
        mixed_rows,
        attended_self,
        logs_self,
        after_self,
        normed_feed,
        average_self,
        inverse_self,
        average_feed,
        inverse_feed,
    ) = self_forward(
        after_cross,
        alive_rows,
        self_gain,
        feed_gain,
        mixed_weight,
        output_weight,
        heads,
        heads_block,
        scale,
    )
    order.mark(normed_feed)
    for step in range(1, tp_count):
        grad_pieces[step] = list(order.hold(tuple(grad_pieces[step])))
    order.mark(normed_feed, *[part for parts in grad_pieces for part in parts])

    feed_pieces = [[] for _ in range(tp_count)]
    for piece in pieces(order.hold(normed_feed)):
        for step in range(1, tp_count):
            feed_pieces[step].append(from_peer(piece, step))
    *filled_parts, grad_normed_feed = feed_block(
        0,
        rows_dev * tp_count,
        order.hold(normed_feed),
        grad_own,
        feed_up,
        feed_down,
        (),
        jnp.float32,
    )
    order.mark(*filled_parts)
    normed_terms = [[] for _ in range(tp_count)]
    for step in range(1, tp_count):
        for place, start in enumerate(piece_starts):
            *filled_parts, term = feed_block(
                step * rows_dev + start,
                rows_dev * tp_count,
                order.hold(feed_pieces[step][place]),
                grad_pieces[step][place],
                feed_up,
                feed_down,
                filled_parts,
                jnp.bfloat16,
            )
            normed_terms[step].append(to_peer(term, step))
            order.mark(term)
    activated, grad_hidden = filled_parts
    feed_all = jnp.concatenate(
        [normed_feed] + [piece for parts in feed_pieces for piece in parts], axis=0
    )
    grad_all = jnp.concatenate(
        [grad_own] + [piece for parts in grad_pieces for piece in parts], axis=0
    )
    received = [[] for _ in range(tp_count)]
    for place in range(len(piece_starts)):
        terms = order.hold(tuple(normed_terms[step][place] for step in range(1, tp_count)))
        for step in range(1, tp_count):
            received[step].append(terms[step - 1])
        order.mark(*terms)
        if place == 0:
            held = order.hold(grad_hidden)
            grad_up = [
                transposed_times(feed_all, held[:, start : start + feed_width]).astype(jnp.bfloat16)
                for start in range(0, hidden_width, feed_width)
            ]
            order.mark(*grad_up)
    grad_down = transposed_times(order.hold(activated), grad_all).astype(jnp.bfloat16)
    if hidden_width >= model:
        grad_down = grad_down.reshape(hidden_width // model, model, model)
    else:
        grad_down = stack_output(grad_down)[None]
    feed_term = jnp.concatenate([jnp.stack(grad_up), grad_down], axis=0)
    order.mark(feed_term)
    feed_share = lax.psum_scatter(feed_term, "sets", scatter_dimension=1, tiled=True)
    for step in range(1, tp_count):
        term = jnp.concatenate(received[step], axis=0)
        grad_normed_feed = order.hold(grad_normed_feed) + term.astype(jnp.float32)
    order.mark(grad_normed_feed)
    average_self, inverse_self, average_feed, inverse_feed = order.hold(
        (average_self, inverse_self, average_feed, inverse_feed)
    )
    unit_feed = (after_self - average_feed) * inverse_feed
    unit_self = (after_cross - average_self) * inverse_self
    grad_rows, grad_feed_gain = norm_backward(
        order.hold(grad_normed_feed), unit_feed, inverse_feed, feed_gain
    )
    grad_after_self = grad_final + grad_rows

    grad_branch = (alive_rows * grad_after_self).astype(jnp.bfloat16)
    grad_attended = times_transposed(grad_branch, output_weight).astype(jnp.bfloat16)
    grad_mixed = self_backward(mixed_rows, grad_attended, logs_self, heads, heads_block, scale)
    order.mark(grad_mixed)
    grad_normed_self = times_transposed(order.hold(grad_mixed), mixed_weight)
    grad_rows, grad_self_gain = norm_backward(grad_normed_self, unit_self, inverse_self, self_gain)
    grad_after_cross = grad_after_self + grad_rows
    grad_cross_blocks = gather_blocks((alive_rows * grad_after_cross).astype(jnp.bfloat16))
    order.mark(grad_cross_blocks[0])

    late_mixed = order.hold(grad_mixed)
    self_terms = []
    for step in range(tp_count):
        terms = [
            transposed_times(
                normed_self, late_mixed[:, (3 * step + kind) * width : (3 * step + kind + 1) * width]
            ).astype(jnp.bfloat16)
            for kind in range(3)
        ]
        output_term = transposed_times(
            attended_self[:, step * width : (step + 1) * width], grad_branch
        ).astype(jnp.bfloat16)
        self_terms.append(terms + [stack_output(output_term)])
    self_sums = [
        SetSum(
            order,
            order.hold(jnp.stack([jnp.stack(terms[first : first + 2]) for terms in self_terms])),
            halve,
            layout=natural,
            peers_after=peers_after,
            double=False,
        )
        for first, halve, peers_after in ((0, bits, 1), (2, bits, len(bits)))
    ]

    grad_queries, sums = [], ()
    for step in range(tp_count):
        block = order.hold(grad_cross_blocks[step])
        grad_attended = times_transposed(block, cross_output).astype(jnp.bfloat16)
        grad_query, *sums = cross_backward(
            log_counts,
            queries_cross[step],
            grad_attended,
            logs_cross[step],
            key_table,
            key_table_t,
            value_table,
            scale,
            step * local_groups,
            tuple(sums),
            step == tp_count - 1,
        )
        grad_queries.append(grad_query)
        order.mark(grad_query)
        if step == 0:
            self_sums[1].advance()
            self_sums[0].advance()
    grad_key_table, grad_value_table = sums
    held_keys, held_values = order.hold((grad_key_table, grad_value_table))
    grad_key = transposed_times(embedded, held_keys).astype(jnp.bfloat16)
    grad_value = transposed_times(embedded, held_values).astype(jnp.bfloat16)
    first_sum = SetSum(order, jnp.stack([grad_key, grad_value]), bits)
    self_sums[1].advance()
    self_sums[0].advance()
    output_terms, query_terms = [], []
    for step in range(tp_count):
        output_terms.append(
            transposed_times(attended_cross[step], order.hold(grad_cross_blocks[step]))
        )
        query_terms.append(transposed_times(rows_cross[step], order.hold(grad_queries[step])))
    grad_query = functools.reduce(jnp.add, query_terms).astype(jnp.bfloat16)
    grad_output = functools.reduce(jnp.add, output_terms).astype(jnp.bfloat16)
    second_sum = SetSum(
        order, order.hold(jnp.stack([grad_query, stack_output(grad_output)])), cross_first
    )
    first_sum.advance()
    feed_share = order.hold(feed_share)
    order.mark(feed_share, *order.last)
    feed_result = lax.all_gather(feed_share, "sets", axis=1, tiled=True)
    second_sum.advance()

    def query_term(step):
        return times_transposed(order.hold(grad_queries[step]), cross_query)

    def input_term(step):
        keys, values = order.hold(
            (table_part(grad_key_table, step), table_part(grad_value_table, step))
        )
        return times_transposed(keys, cross_key) + times_transposed(values, cross_value)

    query_sums, input_sums, final_terms = [], [], []
    for step in range(1, tp_count):
        term = query_term(step).astype(jnp.bfloat16)
        query_sums.append(to_peer(term, step))
        order.mark(term)
    grad_normed_cross = query_term(0)
    order.mark(grad_normed_cross)
    def advance_all(*totals):
        for total in totals:
            total.advance()

    final_all = project(order.hold(activated), feed_down)
    for step in range(1, tp_count):
        term = block_rows(final_all, step).astype(jnp.bfloat16)
        final_terms.append(to_peer(term, step))
        order.mark(term)
    advance_all(self_sums[1], self_sums[0], first_sum, second_sum)
    for step in range(1, tp_count):
        term = input_term(step).astype(jnp.bfloat16)
        input_sums.append(to_peer(term, step))
        order.mark(term)
    advance_all(self_sums[1], self_sums[0], first_sum, second_sum)
    for term in order.hold(tuple(query_sums)):
        grad_normed_cross = grad_normed_cross + term.astype(jnp.float32)
    grad_rows, grad_cross_gain = norm_backward(
        grad_normed_cross, unit_cross, inverse_cross, cross_gain
    )
    latent_grad = grad_after_cross + grad_rows
    order.mark(latent_grad)
    while any(total.stages for total in self_sums):
        advance_all(self_sums[1], self_sums[0])
    self_result = lax.all_gather(
        jnp.concatenate([total.block for total in self_sums], axis=0), "sets", axis=1, tiled=True
    )
    final_rows = block_rows(final_all, 0)
    for term in order.hold(tuple(final_terms)):
        final_rows = final_rows + term.astype(jnp.float32)
    final_rows = after_self + alive_rows * final_rows
    group_rms = jnp.sqrt(jnp.mean((final_rows * final_rows).reshape(local_groups, -1), axis=1))
    penalty_term = jnp.sum(group_rms * group_alive)
    order.mark(final_rows)
    small = jnp.stack(
        [
            grad_feed_gain,
            grad_self_gain,
            jnp.full_like(grad_feed_gain, penalty_term),
            grad_cross_gain,
        ],
        axis=0,
    )
    spots = [("sets", 1 << bit) for bit in bits]
    step = 1
    while step < tp_count:
        spots.append(("tp", step))
        step *= 2

    def small_step():
        nonlocal small
        if spots:
            axis, step = spots.pop(0)
            received = lax.ppermute(
                small, axis, [(place, place ^ step) for place in range(lax.axis_size(axis))]
            )
            small = small + order.hold(received)
            order.mark(small)

    running = [first_sum, second_sum]
    advance_all(*running)
    small_step()
    up_blocks = hidden_width // feed_width
    feed_result = order.hold(feed_result)
    grad_feed_up = jnp.concatenate(
        [feed_result[place] for place in range(up_blocks)], axis=1
    ).astype(jnp.float32)
    if hidden_width >= model:
        grad_feed_down = feed_result[up_blocks:].reshape(hidden_width, model).astype(jnp.float32)
    else:
        grad_feed_down = unstack_output(feed_result[up_blocks]).astype(jnp.float32)
    order.mark(grad_feed_up, grad_feed_down)
    advance_all(*running)
    small_step()
    input_grad = input_term(0)
    for term in order.hold(tuple(input_sums)):
        input_grad = input_grad + term.astype(jnp.float32)
    order.mark(input_grad)
    while any(total.stages for total in running) or spots:
        advance_all(*running)
        small_step()
    grad_self_query, grad_self_key, grad_self_value = [
        self_result[kind].astype(jnp.float32) for kind in range(3)
    ]
    grad_self_output = unstack_output(self_result[3]).astype(jnp.float32)
    grad_cross_key, grad_cross_value = first_sum.result(0), first_sum.result(1)
    grad_cross_query = second_sum.result(0)
    grad_cross_output = unstack_output(second_sum.result(1))
    grad_feed_gain, grad_self_gain, _, grad_cross_gain = [small[place] for place in range(4)]
    penalty = small[2, 0] / (group_count * lax.axis_size("sets"))
    return (
        final_rows.astype(jnp.bfloat16),
        latent_grad,
        input_grad,
        grad_cross_gain,
        grad_cross_query,
        grad_cross_key,
        grad_cross_value,
        grad_cross_output,
        grad_self_gain,
        grad_self_query,
        grad_self_key,
        grad_self_value,
        grad_self_output,
        grad_feed_gain,
        grad_feed_up,
        grad_feed_down,
        penalty,
    )


def solution(mesh):
    return jax.shard_map(
        local,
        mesh=mesh,
        in_specs=(
            P(("sets", "tp"), None),
            P(("sets", "tp"), None),
            P("sets", None),
            P("sets"),
            P("sets"),
            P(("sets", "tp"), None),
            P(),
            P(None, "tp"),
            P(None, "tp"),
            P(None, "tp"),
            P("tp", None),
            P(),
            P(None, "tp"),
            P(None, "tp"),
            P(None, "tp"),
            P("tp", None),
            P(),
            P(None, "tp"),
            P("tp", None),
        ),
        out_specs=(
            P(("sets", "tp"), None),
            P(("sets", "tp"), None),
            P(("sets", "tp"), None),
            P(),
            P(None, "tp"),
            P(None, "tp"),
            P(None, "tp"),
            P("tp", None),
            P(),
            P(None, "tp"),
            P(None, "tp"),
            P(None, "tp"),
            P("tp", None),
            P(),
            P(None, "tp"),
            P("tp", None),
            P(),
        ),
        check_vma=False,
    )
```

```python
import functools
import math

import jax
import jax.numpy as jnp
from jax import lax
from jax.experimental import pallas as pl
from jax.experimental.pallas import tpu as pltpu
from jax.sharding import PartitionSpec as P

HEAD_DIM = 128
GROUP = 128

epsilon = 1e-05
masked_score = -1e30
gelu_factor = 0.7978845608028654
gelu_cubic = 0.044715
log2_e = 1.4426950408889634
vmem_bytes = 60 * 1024 * 1024
small_cost = pl.CostEstimate(flops=1000000, transcendentals=1000, bytes_accessed=100000)


def project(left_rows, right_rows):
    return jnp.dot(left_rows, right_rows, preferred_element_type=jnp.float32)


def times_transposed(left_rows, right_rows):
    return lax.dot_general(
        left_rows, right_rows, (((1,), (1,)), ((), ())), preferred_element_type=jnp.float32
    )


def transposed_times(left_rows, right_rows):
    return lax.dot_general(
        left_rows, right_rows, (((0,), (0,)), ((), ())), preferred_element_type=jnp.float32
    )


def norm_forward(values, gain):
    average = jnp.mean(values, axis=1, keepdims=True)
    centred = values - average
    variance = jnp.mean(centred * centred, axis=1, keepdims=True)
    inverse = lax.rsqrt(variance + epsilon)
    unit_rows = centred * inverse
    return (unit_rows, inverse, (unit_rows * gain).astype(jnp.bfloat16))


def norm_backward(grad_normed, unit_rows, inverse, gain):
    scaled = grad_normed * gain
    first_mean = jnp.mean(scaled, axis=1, keepdims=True)
    second_mean = jnp.mean(scaled * unit_rows, axis=1, keepdims=True)
    grad_rows = inverse * (scaled - first_mean - unit_rows * second_mean)
    return (grad_rows, jnp.sum(grad_normed * unit_rows, axis=0))


def from_peer(block, step):
    count = lax.axis_size("tp")
    return lax.ppermute(block, "tp", [(source, (source - step) % count) for source in range(count)])


def to_peer(block, step):
    count = lax.axis_size("tp")
    return lax.ppermute(block, "tp", [(source, (source + step) % count) for source in range(count)])


def gather_blocks(block):
    return [block] + [from_peer(block, step) for step in range(1, lax.axis_size("tp"))]


def sum_blocks(make_partial):
    received = [
        to_peer(make_partial(step).astype(jnp.bfloat16), step)
        for step in range(1, lax.axis_size("tp"))
    ]
    total = make_partial(0)
    for term in received:
        total = total + term.astype(jnp.float32)
    return total


def swap_sets(block, bit):
    count = lax.axis_size("sets")
    return lax.ppermute(block, "sets", [(source, source ^ (1 << bit)) for source in range(count)])


def set_bit(bit):
    return (lax.axis_index("sets") >> bit) & 1


def halves(block, bit, before=0):
    rows, columns = block.shape[-2:]
    lead = block.shape[:-2]
    view = block.reshape(lead + (2**before, 2, rows // 2 ** (before + 1), columns))
    axis = view.ndim - 3
    mine = set_bit(bit)
    kept, sent = [
        lax.dynamic_slice_in_dim(view, place, 1, axis).reshape(lead + (rows // 2, columns))
        for place in (mine, 1 - mine)
    ]
    return (kept, sent)


def add_pair(kept, received):
    return (kept.astype(jnp.float32) + received.astype(jnp.float32)).astype(jnp.bfloat16)


class Order:
    def __init__(self):
        self.last = ()

    def hold(self, value):
        if not self.last:
            return value
        return lax.optimization_barrier((value, *self.last))[0]

    def mark(self, *values):
        self.last = values


def join(block, received, bit):
    first = set_bit(bit) == 0
    return jnp.concatenate(
        [jnp.where(first, block, received), jnp.where(first, received, block)],
        axis=block.ndim - 2,
    )


def all_bits():
    return list(range(int(math.log2(lax.axis_size("sets")))))


class SetSum:
    def __init__(self, order, block, halve, layout=None, peers_after=None, double=True):
        self.order = order
        self.block = block.astype(jnp.bfloat16)
        self.layout = list(halve if layout is None else layout)
        self.stages = [("halve", bit) for bit in halve]
        if peers_after is not None:
            self.stages.insert(peers_after, ("peers", None))
        if double:
            self.stages += [("double", bit) for bit in reversed(halve)]
        self.last = None
        self.send()

    def send(self):
        kind, bit = self.stages[0]
        if kind == "halve":
            before = self.layout.index(bit)
            self.layout.remove(bit)
            self.kept, sent = halves(self.block, bit, before)
            self.received = [swap_sets(sent, bit)]
        elif kind == "peers":
            self.kept = self.block[0]
            sent = [self.block[step] for step in range(1, self.block.shape[0])]
            self.received = [to_peer(part, step + 1) for step, part in enumerate(sent)]
            self.order.mark(*sent)
            return
        else:
            self.kept = sent = self.block
            self.received = [swap_sets(sent, bit)]
        self.order.mark(sent)

    def advance(self):
        if not self.stages:
            return
        kind, bit = self.stages.pop(0)
        received = self.order.hold(tuple(self.received))
        if kind == "double" and not self.stages:
            self.last = (self.kept, received[0], bit)
            self.order.mark(received[0])
            return
        if kind == "double":
            self.block = join(self.kept, received[0], bit)
        else:
            total = self.kept.astype(jnp.float32)
            for term in received:
                total = total + term.astype(jnp.float32)
            self.block = total.astype(jnp.bfloat16)
        if self.stages:
            self.send()
        else:
            self.order.mark(self.block)

    def result(self, place=None):
        kept, received, bit = self.last
        if place is not None:
            kept, received = kept[place], received[place]
        return join(kept, received, bit).astype(jnp.float32)


def stack_output(weight):
    width = weight.shape[0]
    return jnp.concatenate(
        [weight[:, start : start + width] for start in range(0, weight.shape[1], width)], axis=0
    )


def unstack_output(stacked):
    width = stacked.shape[1]
    return jnp.concatenate(
        [stacked[start : start + width] for start in range(0, stacked.shape[0], width)], axis=1
    )


def multiplicity_kernel(chosen_ref, out_ref):
    row_count = out_ref.shape[0]
    group_count, key_count = chosen_ref.shape
    row_ids = lax.broadcasted_iota(jnp.int32, (row_count, key_count), 0) + (
        pl.program_id(0) * row_count
    )
    lanes = lax.broadcasted_iota(jnp.int32, (key_count, 128), 1)

    def one_group(group, total):
        picked = chosen_ref[pl.ds(group, 1), :]
        hits = jnp.where(row_ids == picked, 1.0, 0.0).astype(jnp.bfloat16)
        place = jnp.where(lanes == group, 1.0, 0.0).astype(jnp.bfloat16)
        return total + project(hits, place)

    total = lax.fori_loop(0, group_count, one_group, jnp.zeros((row_count, 128), jnp.float32))
    out_ref[...] = jnp.where(total > 0.0, jnp.log2(jnp.maximum(total, 1.0)), masked_score)


def log_multiplicity(chosen, counts, table_rows):
    group_count, key_count = chosen.shape
    valid = jnp.arange(key_count, dtype=jnp.int32)[None, :] < counts[:, None]
    chosen = jnp.where(valid, chosen, -1)
    block = math.gcd(table_rows, 512)
    return pl.pallas_call(
        multiplicity_kernel,
        grid=(table_rows // block,),
        in_specs=[pl.BlockSpec((group_count, key_count), lambda i: (0, 0))],
        out_specs=pl.BlockSpec((block, 128), lambda i: (i, 0)),
        out_shape=jax.ShapeDtypeStruct((table_rows, 128), jnp.float32),
        name="multiplicity",
    )(chosen)


def fill_bias(counts_ref, bias_ref, span, first_group):
    row_count = bias_ref.shape[0]
    lanes = lax.broadcasted_iota(jnp.int32, (row_count, 128), 1)
    counts = counts_ref[...]
    for part in range(span):
        group = first_group + pl.program_id(0) * span + part
        column = jnp.sum(jnp.where(lanes == group, counts, 0.0), axis=1, keepdims=True)
        bias_ref[:, part * GROUP : (part + 1) * GROUP] = jnp.broadcast_to(
            column, (row_count, GROUP)
        )


def cross_forward_kernel(
    counts_ref,
    rows_ref,
    key_ref,
    value_t_ref,
    query_weight_ref,
    output_weight_ref,
    query_ref,
    out_ref,
    log_ref,
    branch_ref,
    bias_ref,
    *,
    heads,
    span,
    scale,
    first_group,
):
    fill_bias(counts_ref, bias_ref, span, first_group)
    query_ref[...] = project(rows_ref[...], query_weight_ref[...]).astype(jnp.bfloat16)
    for head in range(heads):
        cols = slice(head * HEAD_DIM, (head + 1) * HEAD_DIM)
        scores = times_transposed(key_ref[:, cols], query_ref[:, cols])
        scores = scores * (scale * log2_e) + bias_ref[...]
        top = jnp.max(scores, axis=0, keepdims=True)
        raised = jnp.exp2(scores - top)
        total = jnp.sum(raised, axis=0, keepdims=True)
        mixed = project(value_t_ref[cols, :], raised.astype(jnp.bfloat16)) / total
        out_ref[:, cols] = mixed.T.astype(jnp.bfloat16)
        log_ref[0, head : head + 1, :] = top + jnp.log2(total)
    branch_ref[...] = project(out_ref[...], output_weight_ref[...]).astype(branch_ref.dtype)


def cross_forward(
    log_counts,
    normed,
    key_table,
    value_table_t,
    query_weight,
    output_weight,
    scale,
    first_group,
    branch_type,
):
    row_count, model = normed.shape
    table_rows, width = key_table.shape
    heads = width // HEAD_DIM
    groups = row_count // GROUP
    span = 2 if groups % 2 == 0 else 1
    rows = span * GROUP
    block = pl.BlockSpec((rows, width), lambda i: (i, 0))
    wide_block = pl.BlockSpec((rows, model), lambda i: (i, 0))
    return pl.pallas_call(
        functools.partial(
            cross_forward_kernel, heads=heads, span=span, scale=scale, first_group=first_group
        ),
        grid=(groups // span,),
        in_specs=[
            pl.BlockSpec((table_rows, 128), lambda i: (0, 0)),
            wide_block,
            pl.BlockSpec((table_rows, width), lambda i: (0, 0)),
            pl.BlockSpec((width, table_rows), lambda i: (0, 0)),
            pl.BlockSpec((model, width), lambda i: (0, 0)),
            pl.BlockSpec((width, model), lambda i: (0, 0)),
        ],
        out_specs=[block, block, pl.BlockSpec((1, heads, rows), lambda i: (i, 0, 0)), wide_block],
        out_shape=[
            jax.ShapeDtypeStruct((row_count, width), jnp.bfloat16),
            jax.ShapeDtypeStruct((row_count, width), jnp.bfloat16),
            jax.ShapeDtypeStruct((groups // span, heads, rows), jnp.float32),
            jax.ShapeDtypeStruct((row_count, model), branch_type),
        ],
        scratch_shapes=[pltpu.VMEM((table_rows, rows), jnp.float32)],
        compiler_params=pltpu.CompilerParams(vmem_limit_bytes=vmem_bytes),
        cost_estimate=small_cost,
        name="cross_forward",
    )(log_counts, normed, key_table, value_table_t, query_weight, output_weight)


def cross_backward_kernel(*refs, heads, span, scale, first_group, start, finish):
    counts_ref, query_ref, grad_ref, log_ref, key_ref, key_t_ref, value_ref = refs[:7]
    refs = refs[7:]
    if not start:
        key_start_ref, value_start_ref = refs[:2]
        refs = refs[2:]
    grad_query_ref, grad_key_ref, grad_value_ref, bias_ref = refs[:4]
    key_sum_ref, value_sum_ref = refs[4:] if finish else (grad_key_ref, grad_value_ref)
    step = pl.program_id(0)

    @pl.when(step == 0)
    def _():
        if start:
            key_sum_ref[...] = jnp.zeros_like(key_sum_ref)
            value_sum_ref[...] = jnp.zeros_like(value_sum_ref)
        else:
            key_sum_ref[...] = key_start_ref[...]
            value_sum_ref[...] = value_start_ref[...]

    fill_bias(counts_ref, bias_ref, span, first_group)
    for head in range(heads):
        cols = slice(head * HEAD_DIM, (head + 1) * HEAD_DIM)
        query = query_ref[:, cols]
        grad = grad_ref[:, cols]
        scores = times_transposed(key_ref[:, cols], query)
        weights = jnp.exp2(
            scores * (scale * log2_e) + bias_ref[...] - log_ref[0, head : head + 1, :]
        )
        grad_weights = times_transposed(value_ref[:, cols], grad)
        inner = jnp.sum(weights * grad_weights, axis=0, keepdims=True)
        grad_scores = (weights * (grad_weights - inner)).astype(jnp.bfloat16)
        value_sum_ref[:, cols] += project(weights.astype(jnp.bfloat16), grad)
        key_sum_ref[:, cols] += project(grad_scores, query)
        grad_query = project(key_t_ref[cols, :], grad_scores) * scale
        grad_query_ref[:, cols] = grad_query.T.astype(jnp.bfloat16)

    if finish:

        @pl.when(step == pl.num_programs(0) - 1)
        def _():
            grad_key_ref[...] = (key_sum_ref[...] * scale).astype(jnp.bfloat16)
            grad_value_ref[...] = value_sum_ref[...].astype(jnp.bfloat16)


def cross_backward(
    log_counts,
    queries,
    grad_attended,
    logs,
    key_table,
    key_table_t,
    value_table,
    scale,
    first_group,
    earlier,
    finish,
):
    row_count, width = queries.shape
    table_rows = key_table.shape[0]
    heads = width // HEAD_DIM
    groups = row_count // GROUP
    span = 2 if groups % 2 == 0 else 1
    rows = span * GROUP
    whole = pl.BlockSpec((table_rows, width), lambda i: (0, 0))
    block = pl.BlockSpec((rows, width), lambda i: (i, 0))
    table_type = jnp.bfloat16 if finish else jnp.float32
    sums = pltpu.VMEM((table_rows, width), jnp.float32)
    return pl.pallas_call(
        functools.partial(
            cross_backward_kernel,
            heads=heads,
            span=span,
            scale=scale,
            first_group=first_group,
            start=not earlier,
            finish=finish,
        ),
        grid=(groups // span,),
        in_specs=[
            pl.BlockSpec((table_rows, 128), lambda i: (0, 0)),
            block,
            block,
            pl.BlockSpec((1, heads, rows), lambda i: (i, 0, 0)),
            whole,
            pl.BlockSpec((width, table_rows), lambda i: (0, 0)),
            whole,
        ]
        + [whole] * len(earlier),
        out_specs=[block, whole, whole],
        out_shape=[
            jax.ShapeDtypeStruct((row_count, width), jnp.bfloat16),
            jax.ShapeDtypeStruct((table_rows, width), table_type),
            jax.ShapeDtypeStruct((table_rows, width), table_type),
        ],
        scratch_shapes=[pltpu.VMEM((table_rows, rows), jnp.float32)]
        + ([sums, sums] if finish else []),
        compiler_params=pltpu.CompilerParams(vmem_limit_bytes=vmem_bytes),
        cost_estimate=small_cost,
        name="cross_backward",
    )(log_counts, queries, grad_attended, logs, key_table, key_table_t, value_table, *earlier)


def head_columns(head, heads_block):
    base = (head // heads_block) * 3 * heads_block + head % heads_block
    return [
        slice((base + kind * heads_block) * HEAD_DIM, (base + kind * heads_block + 1) * HEAD_DIM)
        for kind in range(3)
    ]


def norm_block(values, gain, average_ref, inverse_ref):
    average = jnp.mean(values, axis=1, keepdims=True)
    centred = values - average
    variance = jnp.mean(centred * centred, axis=1, keepdims=True)
    inverse = lax.rsqrt(variance + epsilon)
    average_ref[...] = average
    inverse_ref[...] = inverse
    return (centred * inverse * gain).astype(jnp.bfloat16)


def self_forward_kernel(
    state_ref,
    alive_ref,
    self_gain_ref,
    feed_gain_ref,
    mixed_weight_ref,
    output_weight_ref,
    normed_ref,
    rows_ref,
    out_ref,
    log_ref,
    after_ref,
    feed_ref,
    self_average_ref,
    self_inverse_ref,
    feed_average_ref,
    feed_inverse_ref,
    *,
    heads,
    heads_block,
    scale,
):
    normed_ref[...] = norm_block(
        state_ref[...], self_gain_ref[...], self_average_ref, self_inverse_ref
    )
    rows_ref[...] = project(normed_ref[...], mixed_weight_ref[...]).astype(jnp.bfloat16)
    columns = [head_columns(head, heads_block) for head in range(heads)]
    for group in range(state_ref.shape[0] // GROUP):
        rows = slice(group * GROUP, (group + 1) * GROUP)
        scores = [
            times_transposed(rows_ref[rows, key_cols], rows_ref[rows, query_cols])
            for query_cols, key_cols, _ in columns
        ]
        weights = []
        for head in range(heads):
            scaled = scores[head] * (scale * log2_e)
            top = jnp.max(scaled, axis=0, keepdims=True)
            raised = jnp.exp2(scaled - top)
            total = jnp.sum(raised, axis=0, keepdims=True)
            weights.append((raised * (1.0 / total)).astype(jnp.bfloat16))
            log_ref[group, head : head + 1, :] = top + jnp.log2(total)
        for head in range(heads):
            mixed = transposed_times(weights[head], rows_ref[rows, columns[head][2]])
            out_ref[rows, head * HEAD_DIM : (head + 1) * HEAD_DIM] = mixed.astype(jnp.bfloat16)
    branch = project(out_ref[...], output_weight_ref[...])
    after_ref[...] = state_ref[...] + alive_ref[...] * branch
    feed_ref[...] = norm_block(
        after_ref[...], feed_gain_ref[...], feed_average_ref, feed_inverse_ref
    )


def self_forward(
    state_rows, alive_rows, self_gain, feed_gain, mixed_weight, output_weight, heads, heads_block, scale
):
    row_count, model = state_rows.shape
    groups = row_count // GROUP
    span = 2 if groups % 2 == 0 else 1
    rows = span * GROUP
    mixed_width = mixed_weight.shape[1]

    def block(width):
        return pl.BlockSpec((rows, width), lambda i: (i, 0))

    def whole(array):
        return pl.BlockSpec(array.shape, lambda i: (0, 0))

    def result(width, kind):
        return jax.ShapeDtypeStruct((row_count, width), kind)

    weights = (self_gain[None], feed_gain[None], mixed_weight, output_weight)
    return pl.pallas_call(
        functools.partial(
            self_forward_kernel, heads=heads, heads_block=heads_block, scale=scale
        ),
        grid=(groups // span,),
        in_specs=[block(model), block(1)] + [whole(array) for array in weights],
        out_specs=[
            block(model),
            block(mixed_width),
            block(heads * HEAD_DIM),
            pl.BlockSpec((span, heads, GROUP), lambda i: (i, 0, 0)),
            block(model),
            block(model),
        ]
        + [block(1)] * 4,
        out_shape=[
            result(model, jnp.bfloat16),
            result(mixed_width, jnp.bfloat16),
            result(heads * HEAD_DIM, jnp.bfloat16),
            jax.ShapeDtypeStruct((groups, heads, GROUP), jnp.float32),
            result(model, jnp.float32),
            result(model, jnp.bfloat16),
        ]
        + [result(1, jnp.float32)] * 4,
        compiler_params=pltpu.CompilerParams(vmem_limit_bytes=vmem_bytes),
        cost_estimate=small_cost,
        name="self_forward",
    )(state_rows, alive_rows, *weights)


def self_backward_kernel(rows_ref, grad_ref, log_ref, out_ref, *, heads, heads_block, scale):
    columns = [head_columns(head, heads_block) for head in range(heads)]
    grads = [slice(head * HEAD_DIM, (head + 1) * HEAD_DIM) for head in range(heads)]
    scores = [
        times_transposed(rows_ref[:, key_cols], rows_ref[:, query_cols])
        for query_cols, key_cols, _ in columns
    ]
    grad_weights = [
        times_transposed(rows_ref[:, columns[head][2]], grad_ref[:, grads[head]])
        for head in range(heads)
    ]
    weights, grad_scores = [], []
    for head in range(heads):
        soft = jnp.exp2(scores[head] * (scale * log2_e) - log_ref[0, head : head + 1, :])
        inner = jnp.sum(soft * grad_weights[head], axis=0, keepdims=True)
        grad_scores.append((soft * (grad_weights[head] - inner)).astype(jnp.bfloat16))
        weights.append(soft.astype(jnp.bfloat16))
    for head in range(heads):
        query_cols, key_cols, value_cols = columns[head]
        out_ref[:, value_cols] = project(weights[head], grad_ref[:, grads[head]]).astype(
            jnp.bfloat16
        )
        out_ref[:, key_cols] = (project(grad_scores[head], rows_ref[:, query_cols]) * scale).astype(
            jnp.bfloat16
        )
        out_ref[:, query_cols] = (
            transposed_times(grad_scores[head], rows_ref[:, key_cols]) * scale
        ).astype(jnp.bfloat16)


def self_backward(mixed_rows, grad_attended, logs, heads, heads_block, scale):
    row_count, width = mixed_rows.shape
    groups = row_count // GROUP
    return pl.pallas_call(
        functools.partial(
            self_backward_kernel, heads=heads, heads_block=heads_block, scale=scale
        ),
        grid=(groups,),
        in_specs=[
            pl.BlockSpec((GROUP, width), lambda i: (i, 0)),
            pl.BlockSpec((GROUP, heads * HEAD_DIM), lambda i: (i, 0)),
            pl.BlockSpec((1, heads, GROUP), lambda i: (i, 0, 0)),
        ],
        out_specs=pl.BlockSpec((GROUP, width), lambda i: (i, 0)),
        out_shape=jax.ShapeDtypeStruct((row_count, width), jnp.bfloat16),
        cost_estimate=small_cost,
        name="self_backward",
    )(mixed_rows, grad_attended, logs)


def feed_kernel(rows_ref, grad_ref, up_ref, down_ref, *rest):
    active_ref, grad_hidden_ref, grad_rows_ref, sum_ref = rest[-4:]
    step = pl.program_id(0)

    @pl.when(step == 0)
    def _():
        sum_ref[...] = jnp.zeros_like(sum_ref)

    hidden = project(rows_ref[...], up_ref[...])
    grad_active = times_transposed(grad_ref[...], down_ref[...])
    square = hidden * hidden
    bend = jnp.tanh(gelu_factor * hidden * (1.0 + gelu_cubic * square))
    half_sum = 0.5 * (1.0 + bend)
    slope = half_sum + (0.5 * gelu_factor) * hidden * (1.0 - bend * bend) * (
        1.0 + (3.0 * gelu_cubic) * square
    )
    grad_hidden = (slope * grad_active).astype(jnp.bfloat16)
    active_ref[...] = (hidden * half_sum).astype(jnp.bfloat16)
    grad_hidden_ref[...] = grad_hidden
    sum_ref[...] += times_transposed(grad_hidden, up_ref[...])

    @pl.when(step == pl.num_programs(0) - 1)
    def _():
        grad_rows_ref[...] = sum_ref[...].astype(grad_rows_ref.dtype)


def feed_block(first_row, total_rows, rows, grads, up, down, earlier, sum_type):
    row_count, width = rows.shape
    hidden_width = up.shape[1]
    tile = math.gcd(hidden_width, 512)
    place = first_row // row_count
    result = jax.ShapeDtypeStruct((total_rows, hidden_width), jnp.bfloat16)
    block = pl.BlockSpec((row_count, tile), lambda i: (place, i))
    whole = pl.BlockSpec((row_count, width), lambda i: (0, 0))
    return pl.pallas_call(
        feed_kernel,
        grid=(hidden_width // tile,),
        in_specs=[
            whole,
            whole,
            pl.BlockSpec((width, tile), lambda i: (0, i)),
            pl.BlockSpec((tile, width), lambda i: (i, 0)),
        ]
        + [pl.BlockSpec(memory_space=pl.ANY)] * len(earlier),
        out_specs=[block, block, whole],
        out_shape=[result, result, jax.ShapeDtypeStruct((row_count, width), sum_type)],
        scratch_shapes=[pltpu.VMEM((row_count, width), jnp.float32)],
        input_output_aliases={4: 0, 5: 1} if earlier else {},
        compiler_params=pltpu.CompilerParams(vmem_limit_bytes=vmem_bytes),
        cost_estimate=small_cost,
        name="feed_hidden",
    )(rows, grads, up, down, *earlier)


def local(
    latents,
    inputs,
    neighbours,
    key_counts,
    filled,
    cotangent,
    cross_gain,
    cross_query,
    cross_key,
    cross_value,
    cross_output,
    self_gain,
    self_query,
    self_key,
    self_value,
    self_output,
    feed_gain,
    feed_up,
    feed_down,
):
    tp_count = lax.axis_size("tp")
    tp_index = lax.axis_index("tp")
    bits = all_bits()
    rows_dev = latents.shape[0]
    table_dev = inputs.shape[0]
    table_rows = table_dev * tp_count
    group_count = neighbours.shape[0]
    local_groups = rows_dev // GROUP
    scale = 1.0 / math.sqrt(HEAD_DIM)
    first_group = tp_index * local_groups
    group_alive = (first_group + jnp.arange(local_groups, dtype=jnp.int32) < filled[0]).astype(
        jnp.float32
    )
    alive_rows = jnp.repeat(group_alive, GROUP)[:, None]

    chosen = jnp.roll(neighbours, -first_group, axis=0)
    counts = jnp.roll(key_counts, -first_group, axis=0)
    chosen = (chosen - tp_index * table_dev) % table_rows
    log_counts = log_multiplicity(chosen, counts, table_rows)

    def block_rows(array, step):
        return array[step * rows_dev : (step + 1) * rows_dev]

    def table_part(array, step):
        return array[step * table_dev : (step + 1) * table_dev]

    heads_block = self_query.shape[1] // HEAD_DIM
    heads = heads_block * tp_count
    width = heads_block * HEAD_DIM
    model = self_query.shape[0]
    hidden_width = feed_up.shape[1]
    feed_width = min(hidden_width, model)
    cross_first = bits[:1] + bits[2:] + bits[1:2]
    natural = list(reversed(bits))
    order = Order()

    piece_rows = rows_dev // 2 if local_groups % 2 == 0 else rows_dev
    piece_starts = list(range(0, rows_dev, piece_rows))

    def pieces(block):
        return [block[start : start + piece_rows] for start in piece_starts]

    peer_inputs = gather_blocks(inputs)
    own_slice = jnp.stack([self_query, self_key, self_value, stack_output(self_output)], axis=0)
    share = model // lax.axis_size("sets")
    own_slice = lax.dynamic_slice_in_dim(own_slice, lax.axis_index("sets") * share, share, 1)
    peer_slices = [from_peer(own_slice, step) for step in range(1, tp_count)]

    state_rows = latents.astype(jnp.float32)
    grad_final = cotangent.astype(jnp.float32)
    grad_own = (alive_rows * grad_final).astype(jnp.bfloat16)
    unit_cross, inverse_cross, normed_cross = norm_forward(state_rows, cross_gain)
    order.mark(normed_cross)
    log_counts = log_multiplicity(order.hold(chosen), counts, table_rows)
    order.mark(log_counts)
    peer_inputs = order.hold(tuple(peer_inputs))
    order.mark(*peer_inputs)
    rows_cross = gather_blocks(normed_cross)
    embedded = jnp.concatenate(peer_inputs, axis=0)
    order.mark(embedded)
    peer_stacks = [
        lax.all_gather(part, "sets", axis=1, tiled=True) for part in order.hold(tuple(peer_slices))
    ]
    key_table = project(order.hold(embedded), cross_key).astype(jnp.bfloat16)
    value_table_t = lax.dot_general(
        cross_value, embedded, (((0,), (1,)), ((), ())), preferred_element_type=jnp.float32
    ).astype(jnp.bfloat16)
    order.mark(key_table, value_table_t)
    grad_pieces = [[] for _ in range(tp_count)]
    queries_cross, attended_cross, logs_cross, cross_terms = [], [], [], []
    for step in range(tp_count):
        rows = order.hold(rows_cross[step])
        order.mark(rows)
        if step == tp_count - 1:
            for peer in range(1, tp_count):
                grad_pieces[peer].append(from_peer(order.hold(pieces(grad_own)[0]), peer))
        queries, attended, logs, term = cross_forward(
            log_counts,
            rows,
            key_table,
            value_table_t,
            cross_query,
            cross_output,
            scale,
            step * local_groups,
            jnp.bfloat16 if step else jnp.float32,
        )
        queries_cross.append(queries)
        attended_cross.append(attended)
        logs_cross.append(logs)
        if step == 0:
            branch = term
            order.mark(attended)
        else:
            cross_terms.append(to_peer(term, step))
            order.mark(term)
        if step == tp_count - 1:
            for peer in range(1, tp_count):
                grad_pieces[peer][0] = order.hold(grad_pieces[peer][0])
            order.mark(term, *[parts[0] for parts in grad_pieces[1:]])
    key_table_t = lax.dot_general(
        cross_key, order.hold(embedded), (((0,), (1,)), ((), ())), preferred_element_type=jnp.float32
    ).astype(jnp.bfloat16)
    value_table = project(order.hold(embedded), cross_value).astype(jnp.bfloat16)
    order.mark(key_table_t, value_table)
    peer_stacks = order.hold(tuple(peer_stacks))
    mixed_weight = jnp.concatenate(
        [self_query, self_key, self_value]
        + [stack[kind] for stack in peer_stacks for kind in range(3)],
        axis=1,
    )
    output_weight = jnp.concatenate(
        [self_output] + [unstack_output(stack[3]) for stack in peer_stacks], axis=0
    )
    mixed_weight, output_weight = lax.optimization_barrier((mixed_weight, output_weight))
    order.mark(mixed_weight, output_weight)
    for term in order.hold(tuple(cross_terms)):
        branch = branch + term.astype(jnp.float32)
    after_cross = state_rows + alive_rows * branch
    order.mark(after_cross)

    for piece in pieces(grad_own)[1:]:
        for step in range(1, tp_count):
            grad_pieces[step].append(from_peer(order.hold(piece), step))
    (
        normed_self,
        mixed_rows,
        attended_self,
        logs_self,
        after_self,
        normed_feed,
        average_self,
        inverse_self,
        average_feed,
        inverse_feed,
    ) = self_forward(
        after_cross,
        alive_rows,
        self_gain,
        feed_gain,
        mixed_weight,
        output_weight,
        heads,
        heads_block,
        scale,
    )
    order.mark(normed_feed)
    for step in range(1, tp_count):
        grad_pieces[step] = list(order.hold(tuple(grad_pieces[step])))
    order.mark(normed_feed, *[part for parts in grad_pieces for part in parts])

    feed_pieces = [[] for _ in range(tp_count)]
    for piece in pieces(order.hold(normed_feed)):
        for step in range(1, tp_count):
            feed_pieces[step].append(from_peer(piece, step))
    *filled_parts, grad_normed_feed = feed_block(
        0,
        rows_dev * tp_count,
        order.hold(normed_feed),
        grad_own,
        feed_up,
        feed_down,
        (),
        jnp.float32,
    )
    order.mark(*filled_parts)
    normed_terms = [[] for _ in range(tp_count)]
    for step in range(1, tp_count):
        for place, start in enumerate(piece_starts):
            *filled_parts, term = feed_block(
                step * rows_dev + start,
                rows_dev * tp_count,
                order.hold(feed_pieces[step][place]),
                grad_pieces[step][place],
                feed_up,
                feed_down,
                filled_parts,
                jnp.bfloat16,
            )
            normed_terms[step].append(to_peer(term, step))
            order.mark(term)
    activated, grad_hidden = filled_parts
    feed_all = jnp.concatenate(
        [normed_feed] + [piece for parts in feed_pieces for piece in parts], axis=0
    )
    grad_all = jnp.concatenate(
        [grad_own] + [piece for parts in grad_pieces for piece in parts], axis=0
    )
    received = [[] for _ in range(tp_count)]
    for place in range(len(piece_starts)):
        terms = order.hold(tuple(normed_terms[step][place] for step in range(1, tp_count)))
        for step in range(1, tp_count):
            received[step].append(terms[step - 1])
        order.mark(*terms)
        if place == 0:
            held = order.hold(grad_hidden)
            grad_up = [
                transposed_times(feed_all, held[:, start : start + feed_width]).astype(jnp.bfloat16)
                for start in range(0, hidden_width, feed_width)
            ]
            order.mark(*grad_up)
    grad_down = transposed_times(order.hold(activated), grad_all).astype(jnp.bfloat16)
    if hidden_width >= model:
        grad_down = grad_down.reshape(hidden_width // model, model, model)
    else:
        grad_down = stack_output(grad_down)[None]
    feed_term = jnp.concatenate([jnp.stack(grad_up), grad_down], axis=0)
    order.mark(feed_term)
    feed_share = lax.psum_scatter(feed_term, "sets", scatter_dimension=1, tiled=True)
    for step in range(1, tp_count):
        term = jnp.concatenate(received[step], axis=0)
        grad_normed_feed = order.hold(grad_normed_feed) + term.astype(jnp.float32)
    order.mark(grad_normed_feed)
    average_self, inverse_self, average_feed, inverse_feed = order.hold(
        (average_self, inverse_self, average_feed, inverse_feed)
    )
    unit_feed = (after_self - average_feed) * inverse_feed
    unit_self = (after_cross - average_self) * inverse_self
    grad_rows, grad_feed_gain = norm_backward(
        order.hold(grad_normed_feed), unit_feed, inverse_feed, feed_gain
    )
    grad_after_self = grad_final + grad_rows

    grad_branch = (alive_rows * grad_after_self).astype(jnp.bfloat16)
    grad_attended = times_transposed(grad_branch, output_weight).astype(jnp.bfloat16)
    grad_mixed = self_backward(mixed_rows, grad_attended, logs_self, heads, heads_block, scale)
    order.mark(grad_mixed)
    grad_normed_self = times_transposed(order.hold(grad_mixed), mixed_weight)
    grad_rows, grad_self_gain = norm_backward(grad_normed_self, unit_self, inverse_self, self_gain)
    grad_after_cross = grad_after_self + grad_rows
    grad_cross_blocks = gather_blocks((alive_rows * grad_after_cross).astype(jnp.bfloat16))
    order.mark(grad_cross_blocks[0])

    late_mixed = order.hold(grad_mixed)
    self_terms = []
    for step in range(tp_count):
        terms = [
            transposed_times(
                normed_self, late_mixed[:, (3 * step + kind) * width : (3 * step + kind + 1) * width]
            ).astype(jnp.bfloat16)
            for kind in range(3)
        ]
        output_term = transposed_times(
            attended_self[:, step * width : (step + 1) * width], grad_branch
        ).astype(jnp.bfloat16)
        self_terms.append(terms + [stack_output(output_term)])
    self_sums = [
        SetSum(
            order,
            order.hold(jnp.stack([jnp.stack(terms[first : first + 2]) for terms in self_terms])),
            halve,
            layout=natural,
            peers_after=peers_after,
            double=False,
        )
        for first, halve, peers_after in ((0, bits, 1), (2, bits, len(bits)))
    ]

    grad_queries, sums = [], ()
    for step in range(tp_count):
        block = order.hold(grad_cross_blocks[step])
        grad_attended = times_transposed(block, cross_output).astype(jnp.bfloat16)
        grad_query, *sums = cross_backward(
            log_counts,
            queries_cross[step],
            grad_attended,
            logs_cross[step],
            key_table,
            key_table_t,
            value_table,
            scale,
            step * local_groups,
            tuple(sums),
            step == tp_count - 1,
        )
        grad_queries.append(grad_query)
        order.mark(grad_query)
        if step == 0:
            self_sums[1].advance()
            self_sums[0].advance()
    grad_key_table, grad_value_table = sums
    held_keys, held_values = order.hold((grad_key_table, grad_value_table))
    grad_key = transposed_times(embedded, held_keys).astype(jnp.bfloat16)
    grad_value = transposed_times(embedded, held_values).astype(jnp.bfloat16)
    first_sum = SetSum(order, jnp.stack([grad_key, grad_value]), bits)
    self_sums[1].advance()
    self_sums[0].advance()
    output_terms, query_terms = [], []
    for step in range(tp_count):
        output_terms.append(
            transposed_times(attended_cross[step], order.hold(grad_cross_blocks[step]))
        )
        query_terms.append(transposed_times(rows_cross[step], order.hold(grad_queries[step])))
    grad_query = functools.reduce(jnp.add, query_terms).astype(jnp.bfloat16)
    grad_output = functools.reduce(jnp.add, output_terms).astype(jnp.bfloat16)
    second_sum = SetSum(
        order, order.hold(jnp.stack([grad_query, stack_output(grad_output)])), cross_first
    )
    first_sum.advance()
    feed_share = order.hold(feed_share)
    order.mark(feed_share, *order.last)
    feed_result = lax.all_gather(feed_share, "sets", axis=1, tiled=True)
    second_sum.advance()

    def query_term(step):
        return times_transposed(order.hold(grad_queries[step]), cross_query)

    def input_term(step):
        keys, values = order.hold(
            (table_part(grad_key_table, step), table_part(grad_value_table, step))
        )
        return times_transposed(keys, cross_key) + times_transposed(values, cross_value)

    query_sums, input_sums, final_terms = [], [], []
    for step in range(1, tp_count):
        term = query_term(step).astype(jnp.bfloat16)
        query_sums.append(to_peer(term, step))
        order.mark(term)
    grad_normed_cross = query_term(0)
    order.mark(grad_normed_cross)
    def advance_all(*totals):
        for total in totals:
            total.advance()

    final_all = project(order.hold(activated), feed_down)
    for step in range(1, tp_count):
        term = block_rows(final_all, step).astype(jnp.bfloat16)
        final_terms.append(to_peer(term, step))
        order.mark(term)
    advance_all(self_sums[1], self_sums[0], first_sum, second_sum)
    for step in range(1, tp_count):
        term = input_term(step).astype(jnp.bfloat16)
        input_sums.append(to_peer(term, step))
        order.mark(term)
    advance_all(self_sums[1], self_sums[0], first_sum, second_sum)
    for term in order.hold(tuple(query_sums)):
        grad_normed_cross = grad_normed_cross + term.astype(jnp.float32)
    grad_rows, grad_cross_gain = norm_backward(
        grad_normed_cross, unit_cross, inverse_cross, cross_gain
    )
    latent_grad = grad_after_cross + grad_rows
    order.mark(latent_grad)
    while any(total.stages for total in self_sums):
        advance_all(self_sums[1], self_sums[0])
    self_result = lax.all_gather(
        jnp.concatenate([total.block for total in self_sums], axis=0), "sets", axis=1, tiled=True
    )
    final_rows = block_rows(final_all, 0)
    for term in order.hold(tuple(final_terms)):
        final_rows = final_rows + term.astype(jnp.float32)
    final_rows = after_self + alive_rows * final_rows
    group_rms = jnp.sqrt(jnp.mean((final_rows * final_rows).reshape(local_groups, -1), axis=1))
    penalty_term = jnp.sum(group_rms * group_alive)
    order.mark(final_rows)
    small = jnp.stack(
        [
            grad_feed_gain,
            grad_self_gain,
            jnp.full_like(grad_feed_gain, penalty_term),
            grad_cross_gain,
        ],
        axis=0,
    )
    spots = [("sets", 1 << bit) for bit in bits]
    step = 1
    while step < tp_count:
        spots.append(("tp", step))
        step *= 2

    def small_step():
        nonlocal small
        if spots:
            axis, step = spots.pop(0)
            received = lax.ppermute(
                small, axis, [(place, place ^ step) for place in range(lax.axis_size(axis))]
            )
            small = small + order.hold(received)
            order.mark(small)

    running = [first_sum, second_sum]
    advance_all(*running)
    small_step()
    up_blocks = hidden_width // feed_width
    feed_result = order.hold(feed_result)
    grad_feed_up = jnp.concatenate(
        [feed_result[place] for place in range(up_blocks)], axis=1
    ).astype(jnp.float32)
    if hidden_width >= model:
        grad_feed_down = feed_result[up_blocks:].reshape(hidden_width, model).astype(jnp.float32)
    else:
        grad_feed_down = unstack_output(feed_result[up_blocks]).astype(jnp.float32)
    order.mark(grad_feed_up, grad_feed_down)
    advance_all(*running)
    small_step()
    input_grad = input_term(0)
    for term in order.hold(tuple(input_sums)):
        input_grad = input_grad + term.astype(jnp.float32)
    order.mark(input_grad)
    while any(total.stages for total in running) or spots:
        advance_all(*running)
        small_step()
    grad_self_query, grad_self_key, grad_self_value = [
        self_result[kind].astype(jnp.float32) for kind in range(3)
    ]
    grad_self_output = unstack_output(self_result[3]).astype(jnp.float32)
    grad_cross_key, grad_cross_value = first_sum.result(0), first_sum.result(1)
    grad_cross_query = second_sum.result(0)
    grad_cross_output = unstack_output(second_sum.result(1))
    grad_feed_gain, grad_self_gain, _, grad_cross_gain = [small[place] for place in range(4)]
    penalty = small[2, 0] / (group_count * lax.axis_size("sets"))
    return (
        final_rows.astype(jnp.bfloat16),
        latent_grad,
        input_grad,
        grad_cross_gain,
        grad_cross_query,
        grad_cross_key,
        grad_cross_value,
        grad_cross_output,
        grad_self_gain,
        grad_self_query,
        grad_self_key,
        grad_self_value,
        grad_self_output,
        grad_feed_gain,
        grad_feed_up,
        grad_feed_down,
        penalty,
    )


def solution(mesh):
    return jax.shard_map(
        local,
        mesh=mesh,
        in_specs=(
            P(("sets", "tp"), None),
            P(("sets", "tp"), None),
            P("sets", None),
            P("sets"),
            P("sets"),
            P(("sets", "tp"), None),
            P(),
            P(None, "tp"),
            P(None, "tp"),
            P(None, "tp"),
            P("tp", None),
            P(),
            P(None, "tp"),
            P(None, "tp"),
            P(None, "tp"),
            P("tp", None),
            P(),
            P(None, "tp"),
            P("tp", None),
        ),
        out_specs=(
            P(("sets", "tp"), None),
            P(("sets", "tp"), None),
            P(("sets", "tp"), None),
            P(),
            P(None, "tp"),
            P(None, "tp"),
            P(None, "tp"),
            P("tp", None),
            P(),
            P(None, "tp"),
            P(None, "tp"),
            P(None, "tp"),
            P("tp", None),
            P(),
            P(None, "tp"),
            P("tp", None),
            P(),
        ),
        check_vma=False,
    )
```
